256 devices in a mesh: slab: 64 (over y, z, core), plane: 4 (over x).
Axes of the slice: x: 4, y: 4, z: 8, core: 2. Of those that a mesh axis runs over, the one named last changes fastest.
Arguments:
- a_blocks: bfloat16 [4, 768, 7, 128, 128], P('plane', 'slab'), may hold values from -0.1875 to 0.1875
- a_cols: int32 [4, 768, 7], P('plane', 'slab'), may hold values from 0 to 767, as said below
- p_blocks: bfloat16 [4, 768, 4, 128, 128], P('plane', 'slab'), may hold values from -0.75 to 0.75
- p_cols: int32 [4, 768, 4], replicated, may hold values from 0 to 255, as said below
- coarse_slot: int32 [64, 4], replicated, may hold values from 0 to 3, each once within a row
Outputs:
- coarse_op: float32 [4, 64, 128, 2560], P('plane', 'slab')
The draws below stay inside these ranges and needn't reach their ends.
Inputs may be any that keep to these rules, and one draw needn't show every extreme that they name: `a_cols`: row g = s*12 + r of column p names 7 distinct block rows of column p, among them g itself; they lie in s*12 to s*12 + 11, or, if r < 4, in the 4 rows just below s*12, or, if r >= 8, in the 4 rows from (s+1)*12 on. `p_cols`: row g = s*12 + r names 4 distinct coarse blocks of s*4 to s*4 + 3, or, if r < 4, also of the 4 blocks before, or, if r >= 8, of the 4 blocks after. `coarse_slot`: each row is a permutation of 0 to 3.
All inputs are finite; a program needn't handle non-finite values.
Results may differ from the reference program's by a relative error of at most 0.0029.
Values may be sent and summed in bfloat16 or wider, within the bound.
No kernel may reach another device: no remote copies, remote signals or barrier semaphores. Data moves between devices by JAX's collectives and lax.ppermute only.
A program may use at most 192 MiB of HBM per device.

```python
import jax
import jax.numpy as jnp
from jax import lax

B = 128
BR = 12
GHOST = 4
KA = 7
KP = 4
CB = 1
PLANES = 4
SLABS = 64
CS = 4
NBS = 768
WIN = 2560


def draw_a_cols(key, part):
    rows = jnp.arange(NBS, dtype=jnp.int32)
    slab = rows // BR
    inner = rows % BR
    cand = jnp.arange(BR + 2 * GHOST, dtype=jnp.int32)
    own = (cand[None, :] >= GHOST) & (cand[None, :] < GHOST + BR)
    lower = (cand[None, :] < GHOST) & (inner[:, None] < GHOST) & (slab[:, None] > 0)
    upper = (cand[None, :] >= GHOST + BR) & (inner[:, None] >= BR - GHOST) & (slab[:, None] < SLABS - 1)
    valid = own | lower | upper
    noise = jax.random.randint(key, (PLANES, NBS, BR + 2 * GHOST), 0, 2 ** 20, dtype=jnp.int32)
    score = noise * 128 + cand[None, None, :]
    score = score + jnp.where(lower | upper, 2 ** 27, 0)[None]
    score = score + jnp.where(cand[None, :] == GHOST + inner[:, None], 2 ** 29, 0)[None]
    score = jnp.where(valid[None], score, -1)
    picked = lax.top_k(score, KA)[1].astype(jnp.int32)
    return (slab[None, :, None] * BR - GHOST + picked).astype(jnp.int32)


def draw_p_cols(key, part):
    rows = jnp.arange(NBS, dtype=jnp.int32)
    slab = rows // BR
    inner = rows % BR
    cand = jnp.arange(3 * CS, dtype=jnp.int32)
    own = (cand[None, :] >= CS) & (cand[None, :] < 2 * CS)
    lower = (cand[None, :] < CS) & (inner[:, None] < GHOST) & (slab[:, None] > 0)
    upper = (cand[None, :] >= 2 * CS) & (inner[:, None] >= BR - GHOST) & (slab[:, None] < SLABS - 1)
    valid = own | lower | upper
    noise = jax.random.randint(key, (PLANES, NBS, 3 * CS), 0, 2 ** 20, dtype=jnp.int32)
    score = jnp.where(valid[None], noise * 64 + cand[None, None, :], -1)
    picked = lax.top_k(score, KP)[1].astype(jnp.int32)
    return ((slab[None, :, None] - 1) * CS + picked).astype(jnp.int32)


def shard_levels(key, extent, split, least, high):
    loudness, own = 1.0, jax.random.fold_in(key, 6)
    for dim, blocks in split:
        heights = jnp.exp(jax.random.uniform(jax.random.fold_in(own, dim), (blocks,), jnp.float32, least / len(split), high / len(split)))
        loudness = loudness * jnp.repeat(heights, extent[dim] // blocks).reshape([-1 if axis == dim else 1 for axis in range(len(extent))])
    return loudness


def bell_draw(own_key, dims, scale, bound, shards=(), held_as=jnp.bfloat16):
    array = scale * jax.random.normal(own_key, dims, jnp.float32)
    if shards:
        array = array * shard_levels(own_key, dims, shards, -0.22, 0.18)
    return jnp.clip(array, -bound, bound).astype(held_as)


def setup_inputs(seed: int = 0) -> dict:
    arg_keys = jax.random.split(jax.random.key(seed), 6)
    a_blocks = bell_draw(arg_keys[0], (PLANES, NBS, KA, B, B), (B * KA) ** -0.5, 0.1875, ((0, 4), (1, 64)))
    a_cols = draw_a_cols(jax.random.fold_in(arg_keys[5], 71), 0)
    p_blocks = bell_draw(arg_keys[2], (PLANES, NBS, KP, B, B), 0.125, 0.75, ((0, 4), (1, 64)))
    p_cols = draw_p_cols(jax.random.fold_in(arg_keys[5], 71), 0)
    coarse_slot = jax.vmap(lambda own: jax.random.permutation(own, CS))(jax.random.split(arg_keys[4], SLABS)).reshape((SLABS, CS)).astype(jnp.int32)
    return {"a_blocks": a_blocks, "a_cols": a_cols, "p_blocks": p_blocks, "p_cols": p_cols, "coarse_slot": coarse_slot}


def window_rows(blocks, cols, slot_table, slab):
    count = blocks.shape[0]
    owner = jnp.clip(cols // CS, 0, SLABS - 1)
    inside = cols % CS
    slot = slot_table[owner, inside]
    place = (cols // CS - slab + 1) * CS + slot
    onehot = (place[:, :, None] == jnp.arange(3 * CS, dtype=jnp.int32)[None, None, :]).astype(jnp.float32)
    dense = jnp.einsum('nkw,nkab->nawb', onehot, blocks.astype(jnp.float32))
    return dense.reshape(count, B, 3 * CS * B).astype(jnp.bfloat16)


def reference(a_blocks, a_cols, p_blocks, p_cols, coarse_slot):
    width = 3 * CS * B
    p_padded = jnp.pad(p_blocks, ((0, 0), (GHOST, GHOST), (0, 0), (0, 0), (0, 0)))
    c_padded = jnp.pad(p_cols, ((0, 0), (GHOST, GHOST), (0, 0)))

    def slab_part(slab):
        start = (slab * BR).astype(jnp.int32)
        near_blocks = lax.dynamic_slice_in_dim(p_padded, start, BR + 2 * GHOST, 1)
        near_cols = lax.dynamic_slice_in_dim(c_padded, start, BR + 2 * GHOST, 1)
        dense = window_rows(near_blocks.reshape(-1, KP, B, B), near_cols.reshape(-1, KP), coarse_slot, slab)
        dense = dense.reshape(PLANES, BR + 2 * GHOST, B, width)
        own_a = lax.dynamic_slice_in_dim(a_blocks, start, BR, 1)
        local = lax.dynamic_slice_in_dim(a_cols, start, BR, 1) - (start - GHOST)
        total = jnp.zeros((PLANES, BR, B, width), jnp.float32)
        for k in range(KA):
            picked = jax.vmap(lambda d, i: d[i])(dense, local[:, :, k])
            total = total + jnp.einsum('prab,prbw->praw', own_a[:, :, k].astype(jnp.float32), picked.astype(jnp.float32))
        product = total.astype(jnp.bfloat16)
        own_rows = dense[:, GHOST:GHOST + BR].reshape(-1, width)
        return lax.dot_general(own_rows, product.reshape(-1, width), (((0,), (0,)), ((), ())), preferred_element_type=jnp.float32)

    parts = lax.map(slab_part, jnp.arange(SLABS, dtype=jnp.int32))
    groups = parts.reshape(SLABS, 3, CS * B, width)
    middle = groups[:, 1]
    empty = jnp.zeros((1, CS * B, width), jnp.float32)
    below = jnp.concatenate([empty, groups[:-1, 2]], axis=0)
    above = jnp.concatenate([groups[1:, 0], empty], axis=0)
    edge = CS * B
    full = jnp.pad(middle, ((0, 0), (0, 0), (edge, edge)))
    full = full + jnp.pad(below, ((0, 0), (0, 0), (0, 2 * edge)))
    full = full + jnp.pad(above, ((0, 0), (0, 0), (2 * edge, 0)))
    full = full.reshape(SLABS, PLANES, CB, B, WIN)
    return jnp.transpose(full, (1, 0, 2, 3, 4)).reshape(PLANES, SLABS * CB, B, WIN)
```

```python
import jax
import jax.numpy as jnp
from jax import lax
from jax.experimental import pallas as pl
from jax.experimental.pallas import tpu as pltpu
from jax.sharding import PartitionSpec as P


GHOST = 4
F32 = jnp.float32
BF16 = jnp.bfloat16
VMEM_LIMIT = 28 * 1024 * 1024
HBM = pl.BlockSpec(memory_space=pltpu.HBM)
VMEM = pl.BlockSpec(memory_space=pltpu.VMEM)
SMEM = pl.BlockSpec(memory_space=pltpu.SMEM)


def dot(a, b):
    return lax.dot_general(a, b, (((1,), (0,)), ((), ())), preferred_element_type=F32)


def dot_t(a, b):
    return lax.dot_general(a, b, (((0,), (0,)), ((), ())), preferred_element_type=F32)


def start_a(acol, a_hbm, dst, rows, first, sem):
    b = a_hbm.shape[-1]
    count = dst.shape[1] // b
    for i, r in enumerate(rows):
        for k in range(a_hbm.shape[1]):
            c = jnp.clip(acol[r, k] - first, 0, count - 1)
            pltpu.make_async_copy(
                a_hbm.at[r, k], dst.at[pl.ds(i * b, b), pl.ds(pl.multiple_of(c * b, b), b)], sem
            ).start()


def place_of(rel, slots, m, r, low, high):
    coarse = slots.shape[1]
    c = jnp.clip(rel[m, r], low, high - 1)
    u = lax.div(c, coarse)
    return u * coarse + slots[u, c - u * coarse]


def start_w(rel, slots, p_hbm, w, rows, first_row, low, high, sem, first=0):
    b = p_hbm.shape[-1]
    for i, r in enumerate(rows):
        for m in range(p_hbm.shape[1]):
            q = place_of(rel, slots, m, r, low, high) - first
            pltpu.make_async_copy(
                p_hbm.at[i, m],
                w.at[pl.ds((r - first_row) * b, b), pl.ds(pl.multiple_of(q * b, b), b)],
                sem,
            ).start()


def wait_all(ref, sem):
    pltpu.make_async_copy(ref, ref, sem).wait()


def clear(ref):
    ref[...] = jnp.zeros(ref.shape, ref.dtype)


def halo_kernel(p_hbm, first, last, sems):
    g = GHOST
    rows = p_hbm.shape[0]
    moves = (
        pltpu.make_async_copy(p_hbm.at[rows - g : rows], last, sems.at[0]),
        pltpu.make_async_copy(p_hbm.at[0:g], first, sems.at[1]),
    )
    for move in moves:
        move.start()
    for move in moves:
        move.wait()


def first_kernel(acol, rel, slots, a_hbm, p_hbm, h0_hbm, l2_hbm, far, a_l, a_h, w, h0_v, l2_v, s_a, s_p, s_o):
    e = far.shape[0]
    g = GHOST
    clear(w.at[0:e, 0 : 2 * e])
    start_w(rel, slots, p_hbm.at[0:g], w, range(g, 2 * g), g, 0, 2 * g, s_p)
    clear(w.at[2 * e : 3 * e, e : 3 * e])
    start_w(rel, slots, p_hbm.at[2 * g : 3 * g], w, range(3 * g, 4 * g), g, g, 3 * g, s_p)
    start_w(rel, slots, p_hbm.at[g : 2 * g], w, range(2 * g, 3 * g), g, g, 2 * g, s_p)
    clear(a_l)
    start_a(acol, a_hbm, a_l, range(0, g), 0, s_a)
    clear(a_h)
    start_a(acol, a_hbm, a_h, range(2 * g, 3 * g), g, s_a)
    wait_all(p_hbm, s_p)
    wait_all(a_hbm.at[0 : 2 * g], s_a)
    low = w[0:e, 0:e]
    high = w[2 * e : 3 * e, 2 * e : 3 * e]
    h0_v[...] = dot(a_h[:, 0:e], low).astype(BF16)
    out_h = pltpu.make_async_copy(h0_v, h0_hbm, s_o.at[0])
    out_h.start()
    l2_v[...] = dot(a_l[:, 3 * e : 4 * e], high).astype(BF16)
    out_l = pltpu.make_async_copy(l2_v, l2_hbm, s_o.at[1])
    out_l.start()
    far[:, 0:e] = dot_t(high, h0_v[...]).astype(BF16)
    far[:, e : 2 * e] = dot_t(low, l2_v[...]).astype(BF16)
    out_h.wait()
    out_l.wait()


def second_kernel(
    acol, rel, slots, a_hbm, p_hbm, below, above, l_hbm, h_hbm, up, down,
    a_l, a_h, w, w_b, w_a, l_v, h_v, s_p, s_b, s_u, s_l, s_h, s_o,
):
    e = up.shape[0]
    g = GHOST
    one, two = slice(0, e), slice(e, 2 * e)
    clear(a_l)
    start_a(acol, a_hbm, a_l, range(0, g), 0, s_l)
    clear(w.at[0:e, 0 : 2 * e])
    start_w(rel, slots, p_hbm.at[0:g], w, range(g, 2 * g), g, 0, 2 * g, s_p)
    clear(w.at[2 * e : 3 * e, e : 3 * e])
    start_w(rel, slots, p_hbm.at[2 * g : 3 * g], w, range(3 * g, 4 * g), g, g, 3 * g, s_p)
    start_w(rel, slots, p_hbm.at[g : 2 * g], w, range(2 * g, 3 * g), g, g, 2 * g, s_p)
    clear(w_b)
    start_w(rel, slots, below, w_b, range(0, g), 0, 0, 2 * g, s_b)
    clear(a_h)
    start_a(acol, a_hbm, a_h, range(2 * g, 3 * g), g, s_h)
    clear(w_a)
    start_w(rel, slots, above, w_a, range(4 * g, 5 * g), 4 * g, g, 3 * g, s_u, g)
    wait_all(a_hbm.at[0:g], s_l)
    wait_all(p_hbm, s_p)
    low = w[0:e, 0:e]
    high = w[2 * e : 3 * e, 2 * e : 3 * e]
    wait_all(below, s_b)
    l_v[:, one] = (dot(a_l[:, 0:e], w_b[:, one]) + dot(a_l[:, e : 2 * e], low)).astype(BF16)
    down[:, one] = dot_t(low, l_v[:, one]).astype(BF16)
    l_v[:, two] = (dot(a_l[:, 0:e], w_b[:, two]) + dot(a_l[:, e : 4 * e], w[:, two])).astype(BF16)
    out_l = pltpu.make_async_copy(l_v, l_hbm, s_o.at[0])
    out_l.start()
    down[:, two] = dot_t(low, l_v[:, two]).astype(BF16)
    wait_all(above, s_u)
    wait_all(a_hbm.at[2 * g : 3 * g], s_h)
    h_v[:, two] = (dot(a_h[:, 2 * e : 3 * e], high) + dot(a_h[:, 3 * e : 4 * e], w_a[:, two])).astype(BF16)
    up[:, two] = dot_t(high, h_v[:, two]).astype(BF16)
    h_v[:, one] = (dot(a_h[:, 0 : 3 * e], w[:, two]) + dot(a_h[:, 3 * e : 4 * e], w_a[:, one])).astype(BF16)
    out_h = pltpu.make_async_copy(h_v, h_hbm, s_o.at[1])
    out_h.start()
    up[:, one] = dot_t(high, h_v[:, one]).astype(BF16)
    out_l.wait()
    out_h.wait()


def third_kernel(
    acol, rel, slots, a_hbm, p_hbm, l_hbm, h_hbm, l2_hbm, h0_hbm, middle, a_m, ap_l, ap_m, ap_h, w, s_p, s_m, s_a
):
    e = a_m.shape[0]
    g = GHOST
    clear(w.at[0:e, 0 : 2 * e])
    start_w(rel, slots, p_hbm.at[0:g], w, range(g, 2 * g), g, 0, 2 * g, s_p)
    clear(w.at[2 * e : 3 * e, e : 3 * e])
    start_w(rel, slots, p_hbm.at[2 * g : 3 * g], w, range(3 * g, 4 * g), g, g, 3 * g, s_p)
    start_w(rel, slots, p_hbm.at[g : 2 * g], w, range(2 * g, 3 * g), g, g, 2 * g, s_p)
    clear(a_m)
    start_a(acol, a_hbm, a_m, range(g, 2 * g), g, s_m)
    moves = [
        pltpu.make_async_copy(src, dst, s_a.at[i])
        for i, (src, dst) in enumerate(
            (
                (l_hbm, ap_l.at[:, 0 : 2 * e]),
                (l2_hbm, ap_l.at[:, 2 * e : 3 * e]),
                (h0_hbm, ap_h.at[:, 0:e]),
                (h_hbm, ap_h.at[:, e : 3 * e]),
            )
        )
    ]
    for move in moves:
        move.start()
    wait_all(p_hbm, s_p)
    wait_all(a_hbm.at[g : 2 * g], s_m)
    ap_m[:, 0:e] = dot(a_m[:, 0:e], w[0:e, 0:e]).astype(BF16)
    ap_m[:, e : 2 * e] = dot(a_m[...], w[:, e : 2 * e]).astype(BF16)
    ap_m[:, 2 * e : 3 * e] = dot(a_m[:, 2 * e : 3 * e], w[2 * e : 3 * e, 2 * e : 3 * e]).astype(BF16)
    for move in moves:
        move.wait()
    w_l = w[0:e, e : 2 * e]
    w_m = w[e : 2 * e, e : 2 * e]
    w_h = w[2 * e : 3 * e, e : 2 * e]
    for c in range(3):
        at = slice(c * e, (c + 1) * e)
        middle[:, at] = dot_t(w_l, ap_l[:, at]) + dot_t(w_m, ap_m[:, at]) + dot_t(w_h, ap_h[:, at])


def fourth_kernel(middle, below, above, near):
    e = near.shape[0]
    one, two, three = (slice(c * e, (c + 1) * e) for c in range(3))
    near[:, one] = (middle[:, one] + below[:, one].astype(F32)).astype(BF16)
    near[:, two] = (middle[:, two] + below[:, two].astype(F32) + above[:, one].astype(F32)).astype(BF16)
    near[:, three] = (middle[:, three] + above[:, two].astype(F32)).astype(BF16)


def run(body, ins, in_specs, outs, out_specs, scratch, flops):
    return pl.pallas_call(
        body,
        in_specs=in_specs,
        out_specs=out_specs,
        out_shape=outs,
        scratch_shapes=scratch,
        compiler_params=pltpu.CompilerParams(vmem_limit_bytes=VMEM_LIMIT),
        cost_estimate=pl.CostEstimate(flops=flops, transcendentals=0, bytes_accessed=8 * 1024 * 1024),
    )(*ins)


def passed_along(shard, by):
    count = lax.axis_size("slab")
    pairs = [(i, i + by) for i in range(count) if 0 <= i + by < count]
    return lax.ppermute(shard, "slab", pairs)


def window_cols(p_cols, coarse_slot, rows_here):
    coarse = coarse_slot.shape[1]
    slab = lax.axis_index("slab")
    column = lax.axis_index("plane")
    turned = jnp.transpose(p_cols, (0, 2, 1))
    mine = lax.dynamic_slice_in_dim(turned, column, 1, 0)[0]
    mine = jnp.pad(mine, ((0, 0), (GHOST, GHOST)))
    near = lax.dynamic_slice_in_dim(mine, slab * rows_here, rows_here + 2 * GHOST, 1)
    slots = jnp.pad(coarse_slot, ((1, 1), (0, 0)))
    return near - (slab - 1) * coarse, lax.dynamic_slice_in_dim(slots, slab, 3, 0)


def steps(a_blocks, a_cols, p_blocks, p_cols, coarse_slot):
    rows_here, b = a_blocks.shape[1], a_blocks.shape[3]
    coarse = coarse_slot.shape[1]
    e = coarse * b
    slab = lax.axis_index("slab")
    a, p = a_blocks[0], p_blocks[0]
    a = pltpu.with_memory_space_constraint(a, pltpu.HBM)
    p_here = pltpu.with_memory_space_constraint(p, pltpu.HBM)
    part = pltpu.VMEM((GHOST, *p.shape[1:]), BF16)
    first, last = run(halo_kernel, (p_here,), [HBM], (part, part), (VMEM, VMEM), [pltpu.SemaphoreType.DMA((2,))], 0)
    below = passed_along(last, 1)
    above = passed_along(first, -1)
    rel, slots = window_cols(p_cols, coarse_slot, rows_here)
    acol = a_cols[0] - (slab * rows_here - GHOST)
    unit = 2 * e * e * b

    def shape(rows, cols, dtype=BF16, space=pltpu.VMEM):
        return space((rows * e, cols * e), dtype)

    def far_shape(rows, cols):
        return shape(rows, cols, BF16, pltpu.HBM)

    a = pltpu.with_memory_space_constraint(a, pltpu.HBM)
    p_here = pltpu.with_memory_space_constraint(p, pltpu.HBM)

    def scratch(rows, cols):
        return pltpu.VMEM((rows * e, cols * e), BF16)

    dma = pltpu.SemaphoreType.DMA(())
    ap_h0, ap_l2, far = run(
        first_kernel,
        (acol, rel, slots, a, p_here),
        [SMEM, SMEM, SMEM, HBM, HBM],
        (far_shape(1, 1), far_shape(1, 1), shape(1, 2)),
        (HBM, HBM, VMEM),
        [scratch(1, 4), scratch(1, 4), scratch(3, 3), scratch(1, 1), scratch(1, 1)]
        + [dma, dma, pltpu.SemaphoreType.DMA((2,))],
        16 * unit,
    )
    far = lax.all_to_all(far.reshape(coarse, 1, b, 2 * e), "plane", 0, 0, tiled=True)
    below, above = (pltpu.with_memory_space_constraint(x, pltpu.VMEM) for x in (below, above))
    ap_l, ap_h, up, down = run(
        second_kernel,
        (acol, rel, slots, a, p_here, below, above),
        [SMEM, SMEM, SMEM, HBM, HBM, VMEM, VMEM],
        (far_shape(1, 2), far_shape(1, 2), shape(1, 2), shape(1, 2)),
        (HBM, HBM, VMEM, VMEM),
        [scratch(1, 4), scratch(1, 4), scratch(3, 3)]
        + [scratch(1, 2)] * 4
        + [dma] * 5
        + [pltpu.SemaphoreType.DMA((2,))],
        64 * unit,
    )
    from_below = passed_along(up, 1)
    from_above = passed_along(down, -1)
    kept = tuple(pltpu.with_memory_space_constraint(x, pltpu.HBM) for x in (ap_l, ap_h, ap_l2, ap_h0))
    middle = run(
        third_kernel,
        (acol, rel, slots, a, p_here) + kept,
        [SMEM, SMEM, SMEM] + [HBM] * 6,
        shape(1, 3, F32),
        VMEM,
        [scratch(1, 3)] * 4 + [scratch(3, 3), dma, dma, pltpu.SemaphoreType.DMA((4,))],
        56 * unit,
    )
    far = jnp.sum(far.astype(F32), axis=0)
    far_low = passed_along(far[:, :, :e], 1)
    far_high = passed_along(far[:, :, e:], -1)
    near = run(fourth_kernel, (middle, from_below, from_above), [VMEM] * 3, shape(1, 3), VMEM, [], e * 3 * e)
    near = near.reshape(coarse, 1, b, 3 * e)
    near = lax.all_to_all(near, "plane", 0, 0, tiled=True)
    near = jnp.sum(near.astype(F32), axis=0)
    return jnp.concatenate([far_low, near, far_high], axis=2)[None]


def solution(mesh):
    return jax.shard_map(
        steps,
        mesh=mesh,
        in_specs=(
            P("plane", "slab", None, None, None),
            P("plane", "slab", None),
            P("plane", "slab", None, None, None),
            P(),
            P(),
        ),
        out_specs=P("plane", "slab", None, None),
        check_vma=False,
    )
```

```python
import jax
import jax.numpy as jnp
from jax import lax
from jax.experimental import pallas as pl
from jax.experimental.pallas import tpu as pltpu
from jax.sharding import PartitionSpec as P


GHOST = 4
F32 = jnp.float32
BF16 = jnp.bfloat16
VMEM_LIMIT = 20 * 1024 * 1024
HBM = pl.BlockSpec(memory_space=pltpu.HBM)
VMEM = pl.BlockSpec(memory_space=pltpu.VMEM)
SMEM = pl.BlockSpec(memory_space=pltpu.SMEM)


def dot(a, b):
    return lax.dot_general(a, b, (((1,), (0,)), ((), ())), preferred_element_type=F32)


def dot_t(a, b):
    return lax.dot_general(a, b, (((0,), (0,)), ((), ())), preferred_element_type=F32)


def start_a(acol, a_hbm, dst, rows, first, sem):
    b = a_hbm.shape[-1]
    count = dst.shape[1] // b
    for i, r in enumerate(rows):
        for k in range(a_hbm.shape[1]):
            c = jnp.clip(acol[r, k] - first, 0, count - 1)
            pltpu.make_async_copy(
                a_hbm.at[r, k], dst.at[pl.ds(i * b, b), pl.ds(pl.multiple_of(c * b, b), b)], sem
            ).start()


def place_of(rel, slots, m, r, low, high):
    coarse = slots.shape[1]
    c = jnp.clip(rel[m, r], low, high - 1)
    u = lax.div(c, coarse)
    return u * coarse + slots[u, c - u * coarse]


def start_w(rel, slots, p_hbm, w, rows, first_row, low, high, sem, first=0):
    b = p_hbm.shape[-1]
    for i, r in enumerate(rows):
        for m in range(p_hbm.shape[1]):
            q = place_of(rel, slots, m, r, low, high) - first
            pltpu.make_async_copy(
                p_hbm.at[i, m],
                w.at[pl.ds((r - first_row) * b, b), pl.ds(pl.multiple_of(q * b, b), b)],
                sem,
            ).start()


def wait_all(ref, sem):
    pltpu.make_async_copy(ref, ref, sem).wait()


def clear(ref):
    ref[...] = jnp.zeros(ref.shape, ref.dtype)


def halo_kernel(p_hbm, first_hbm, last_hbm, first, last, s_i, s_o):
    g = GHOST
    rows = p_hbm.shape[0]
    sides = ((p_hbm.at[rows - g : rows], last, last_hbm), (p_hbm.at[0:g], first, first_hbm))
    moves = []
    for i, (src, here, dst) in enumerate(sides):
        for r in range(g):
            at = i * g + r
            into = pltpu.make_async_copy(src.at[r], here.at[r], s_i.at[at])
            into.start()
            moves.append((into, pltpu.make_async_copy(here.at[r], dst.at[r], s_o.at[at])))
    for into, out in moves:
        into.wait()
        out.start()
    for _, out in moves:
        out.wait()


def first_kernel(
    acol, rel, slots, a_hbm, p_hbm, ghost_l, ghost_h, corner_l, corner_h, own_l, own_h, h0_hbm, l2_hbm, far_hbm,
    a_l, a_h, w, h0_v, l2_v, far, s_p, s_m, s_h, s_l, s_o,
):
    e = far.shape[0]
    g = GHOST
    one, two = slice(0, e), slice(e, 2 * e)
    outs = []

    def send(src, dst):
        outs.append(pltpu.make_async_copy(src, dst, s_o.at[len(outs)]))
        outs[-1].start()

    clear(w.at[0:e, 0 : 2 * e])
    start_w(rel, slots, p_hbm.at[0:g], w, range(g, 2 * g), g, 0, 2 * g, s_p)
    clear(w.at[2 * e : 3 * e, e : 3 * e])
    start_w(rel, slots, p_hbm.at[2 * g : 3 * g], w, range(3 * g, 4 * g), g, g, 3 * g, s_p)
    clear(a_h)
    start_a(acol, a_hbm, a_h, range(2 * g, 3 * g), g, s_h)
    clear(a_l)
    start_a(acol, a_hbm, a_l, range(0, g), 0, s_l)
    start_w(rel, slots, p_hbm.at[g : 2 * g], w, range(2 * g, 3 * g), g, g, 2 * g, s_m)
    wait_all(p_hbm.at[0 : 2 * g], s_p)
    wait_all(a_hbm.at[0:g], s_h)
    low = w[0:e, 0:e]
    high = w[2 * e : 3 * e, 2 * e : 3 * e]
    h0_v[...] = dot(a_h[:, 0:e], low).astype(BF16)
    send(h0_v, h0_hbm)
    far[:, one] = dot_t(high, h0_v[...]).astype(BF16)
    send(far.at[:, one], far_hbm.at[:, one])
    wait_all(a_hbm.at[0:g], s_l)
    l2_v[...] = dot(a_l[:, 3 * e : 4 * e], high).astype(BF16)
    send(l2_v, l2_hbm)
    far[:, two] = dot_t(low, l2_v[...]).astype(BF16)
    send(far.at[:, two], far_hbm.at[:, two])
    corner_l[...] = low
    corner_h[...] = high
    ghost_l[...] = a_l[:, 0:e]
    ghost_h[...] = a_h[:, 3 * e : 4 * e]
    own_l[:, one] = dot(a_l[:, e : 2 * e], low)
    own_h[:, two] = dot(a_h[:, 2 * e : 3 * e], high)
    wait_all(p_hbm.at[0:g], s_m)
    own_l[:, two] = dot(a_l[:, e : 4 * e], w[:, two])
    own_h[:, one] = dot(a_h[:, 0 : 3 * e], w[:, two])
    for out in outs:
        out.wait()


def second_kernel(
    rel, slots, ghost_l, ghost_h, low, high, own_l, own_h, below, above, l_hbm, h_hbm, up_hbm, down_hbm,
    w_b, w_a, l_v, h_v, up, down, s_b, s_u, s_o,
):
    e = up.shape[0]
    g = GHOST
    one, two = slice(0, e), slice(e, 2 * e)
    outs = []

    def send(src, dst):
        outs.append(pltpu.make_async_copy(src, dst, s_o.at[len(outs)]))
        outs[-1].start()

    clear(w_b)
    start_w(rel, slots, below, w_b, range(0, g), 0, 0, 2 * g, s_b)
    clear(w_a)
    start_w(rel, slots, above, w_a, range(4 * g, 5 * g), 4 * g, g, 3 * g, s_u, g)
    wait_all(below, s_b)
    l_v[...] = (own_l[...] + dot(ghost_l[...], w_b[...])).astype(BF16)
    send(l_v, l_hbm)
    down[...] = dot_t(low[...], l_v[...]).astype(BF16)
    send(down, down_hbm)
    wait_all(above, s_u)
    h_v[:, one] = (own_h[:, one] + dot(ghost_h[...], w_a[:, one])).astype(BF16)
    up[:, one] = dot_t(high[...], h_v[:, one]).astype(BF16)
    send(up.at[:, one], up_hbm.at[:, one])
    h_v[:, two] = (own_h[:, two] + dot(ghost_h[...], w_a[:, two])).astype(BF16)
    send(h_v, h_hbm)
    up[:, two] = dot_t(high[...], h_v[:, two]).astype(BF16)
    send(up.at[:, two], up_hbm.at[:, two])
    for out in outs:
        out.wait()


def third_kernel(
    acol, rel, slots, a_hbm, p_hbm, l_hbm, h_hbm, l2_hbm, h0_hbm, middle, a_m, ap_l, ap_m, ap_h, w, s_p, s_m, s_a
):
    e = a_m.shape[0]
    g = GHOST
    clear(w.at[0:e, 0 : 2 * e])
    start_w(rel, slots, p_hbm.at[0:g], w, range(g, 2 * g), g, 0, 2 * g, s_p)
    clear(w.at[2 * e : 3 * e, e : 3 * e])
    start_w(rel, slots, p_hbm.at[2 * g : 3 * g], w, range(3 * g, 4 * g), g, g, 3 * g, s_p)
    start_w(rel, slots, p_hbm.at[g : 2 * g], w, range(2 * g, 3 * g), g, g, 2 * g, s_p)
    clear(a_m)
    start_a(acol, a_hbm, a_m, range(g, 2 * g), g, s_m)
    moves = [
        pltpu.make_async_copy(src, dst, s_a.at[i])
        for i, (src, dst) in enumerate(
            (
                (l_hbm, ap_l.at[:, 0 : 2 * e]),
                (l2_hbm, ap_l.at[:, 2 * e : 3 * e]),
                (h0_hbm, ap_h.at[:, 0:e]),
                (h_hbm, ap_h.at[:, e : 3 * e]),
            )
        )
    ]
    for move in moves:
        move.start()
    wait_all(p_hbm, s_p)
    wait_all(a_hbm.at[g : 2 * g], s_m)
    ap_m[:, 0:e] = dot(a_m[:, 0:e], w[0:e, 0:e]).astype(BF16)
    ap_m[:, e : 2 * e] = dot(a_m[...], w[:, e : 2 * e]).astype(BF16)
    ap_m[:, 2 * e : 3 * e] = dot(a_m[:, 2 * e : 3 * e], w[2 * e : 3 * e, 2 * e : 3 * e]).astype(BF16)
    for move in moves:
        move.wait()
    w_l = w[0:e, e : 2 * e]
    w_m = w[e : 2 * e, e : 2 * e]
    w_h = w[2 * e : 3 * e, e : 2 * e]
    for c in range(3):
        at = slice(c * e, (c + 1) * e)
        middle[:, at] = dot_t(w_l, ap_l[:, at]) + dot_t(w_m, ap_m[:, at]) + dot_t(w_h, ap_h[:, at])


def fourth_kernel(middle, below, above, near_hbm, near, s_o):
    e = near.shape[0]
    one, two, three = (slice(c * e, (c + 1) * e) for c in range(3))
    outs = [pltpu.make_async_copy(near.at[:, c], near_hbm.at[:, c], s_o.at[i]) for i, c in enumerate((one, two, three))]
    near[:, one] = (middle[:, one] + below[:, one].astype(F32)).astype(BF16)
    outs[0].start()
    near[:, two] = (middle[:, two] + below[:, two].astype(F32) + above[:, one].astype(F32)).astype(BF16)
    outs[1].start()
    near[:, three] = (middle[:, three] + above[:, two].astype(F32)).astype(BF16)
    outs[2].start()
    for out in outs:
        out.wait()


def summed_kernel(far, low, high):
    e = low.shape[1]
    low[...] = sum(far[q, :, 0:e].astype(F32) for q in range(far.shape[0]))
    high[...] = sum(far[q, :, e : 2 * e].astype(F32) for q in range(far.shape[0]))


def run(body, ins, in_specs, outs, out_specs, scratch, flops):
    return pl.pallas_call(
        body,
        in_specs=in_specs,
        out_specs=out_specs,
        out_shape=outs,
        scratch_shapes=scratch,
        compiler_params=pltpu.CompilerParams(vmem_limit_bytes=VMEM_LIMIT),
        cost_estimate=pl.CostEstimate(flops=flops, transcendentals=0, bytes_accessed=8 * 1024 * 1024),
    )(*ins)


def passed_along(shard, by):
    count = lax.axis_size("slab")
    pairs = [(i, i + by) for i in range(count) if 0 <= i + by < count]
    return lax.ppermute(shard, "slab", pairs)


def window_cols(p_cols, coarse_slot, rows_here):
    coarse = coarse_slot.shape[1]
    slab = lax.axis_index("slab")
    column = lax.axis_index("plane")
    turned = jnp.transpose(p_cols, (0, 2, 1))
    mine = lax.dynamic_slice_in_dim(turned, column, 1, 0)[0]
    mine = jnp.pad(mine, ((0, 0), (GHOST, GHOST)))
    near = lax.dynamic_slice_in_dim(mine, slab * rows_here, rows_here + 2 * GHOST, 1)
    slots = jnp.pad(coarse_slot, ((1, 1), (0, 0)))
    return near - (slab - 1) * coarse, lax.dynamic_slice_in_dim(slots, slab, 3, 0)


def steps(a_blocks, a_cols, p_blocks, p_cols, coarse_slot):
    rows_here, b = a_blocks.shape[1], a_blocks.shape[3]
    coarse = coarse_slot.shape[1]
    e = coarse * b
    slab = lax.axis_index("slab")
    a, p = a_blocks[0], p_blocks[0]
    a = pltpu.with_memory_space_constraint(a, pltpu.HBM)
    p_here = pltpu.with_memory_space_constraint(p, pltpu.HBM)
    part = pltpu.HBM((GHOST, *p.shape[1:]), BF16)
    first, last = run(
        halo_kernel,
        (p_here,),
        [HBM],
        (part, part),
        (HBM, HBM),
        [pltpu.VMEM(part.shape, BF16)] * 2 + [pltpu.SemaphoreType.DMA((2 * GHOST,))] * 2,
        0,
    )
    below = passed_along(last, 1)
    above = passed_along(first, -1)
    rel, slots = window_cols(p_cols, coarse_slot, rows_here)
    acol = a_cols[0] - (slab * rows_here - GHOST)
    unit = 2 * e * e * b

    def shape(rows, cols, dtype=BF16, space=pltpu.VMEM):
        return space((rows * e, cols * e), dtype)

    def far_shape(rows, cols):
        return shape(rows, cols, BF16, pltpu.HBM)

    a = pltpu.with_memory_space_constraint(a, pltpu.HBM)
    p_here = pltpu.with_memory_space_constraint(p, pltpu.HBM)

    def scratch(rows, cols):
        return pltpu.VMEM((rows * e, cols * e), BF16)

    dma = pltpu.SemaphoreType.DMA(())
    *kept, ap_h0, ap_l2, far = run(
        first_kernel,
        (acol, rel, slots, a, p_here),
        [SMEM, SMEM, SMEM, HBM, HBM],
        (shape(1, 1),) * 4 + (shape(1, 2, F32),) * 2 + (far_shape(1, 1), far_shape(1, 1), far_shape(1, 2)),
        (VMEM,) * 6 + (HBM,) * 3,
        [scratch(1, 4), scratch(1, 4), scratch(3, 3), scratch(1, 1), scratch(1, 1), scratch(1, 2)]
        + [dma] * 4
        + [pltpu.SemaphoreType.DMA((4,))],
        48 * unit,
    )
    far = lax.all_to_all(far.reshape(coarse, 1, b, 2 * e), "plane", 0, 0, tiled=True)
    below, above = (pltpu.with_memory_space_constraint(x, pltpu.VMEM) for x in (below, above))
    ap_l, ap_h, up, down = run(
        second_kernel,
        (rel, slots, *kept, below, above),
        [SMEM, SMEM] + [VMEM] * 8,
        (far_shape(1, 2),) * 4,
        (HBM,) * 4,
        [scratch(1, 2)] * 6 + [dma, dma, pltpu.SemaphoreType.DMA((5,))],
        32 * unit,
    )
    from_below = passed_along(up, 1)
    from_above = passed_along(down, -1)
    kept = tuple(pltpu.with_memory_space_constraint(x, pltpu.HBM) for x in (ap_l, ap_h, ap_l2, ap_h0))
    middle = run(
        third_kernel,
        (acol, rel, slots, a, p_here) + kept,
        [SMEM, SMEM, SMEM] + [HBM] * 6,
        shape(1, 3, F32),
        VMEM,
        [scratch(1, 3)] * 4 + [scratch(3, 3), dma, dma, pltpu.SemaphoreType.DMA((4,))],
        56 * unit,
    )
    near = run(
        fourth_kernel,
        (middle, from_below, from_above),
        [VMEM] * 3,
        far_shape(1, 3),
        HBM,
        [scratch(1, 3), pltpu.SemaphoreType.DMA((3,))],
        e * 3 * e,
    )
    near = near.reshape(coarse, 1, b, 3 * e)
    near = lax.all_to_all(near, "plane", 0, 0, tiled=True)
    one = pltpu.VMEM((b, e), F32)
    low, high = run(summed_kernel, (far.reshape(coarse, b, 2 * e),), [VMEM], (one, one), (VMEM, VMEM), [], b * e * 8)
    far_low = passed_along(low, 1)
    far_high = passed_along(high, -1)
    near = jnp.sum(near.astype(F32), axis=0)
    return jnp.concatenate([far_low[None], near, far_high[None]], axis=2)[None]


def solution(mesh):
    return jax.shard_map(
        steps,
        mesh=mesh,
        in_specs=(
            P("plane", "slab", None, None, None),
            P("plane", "slab", None),
            P("plane", "slab", None, None, None),
            P(),
            P(),
        ),
        out_specs=P("plane", "slab", None, None),
        check_vma=False,
    )
```

```python
import jax
import jax.numpy as jnp
from jax import lax
from jax.experimental import pallas as pl
from jax.experimental.pallas import tpu as pltpu
from jax.sharding import PartitionSpec as P


GHOST = 4
F32 = jnp.float32
BF16 = jnp.bfloat16
VMEM_LIMIT = 20 * 1024 * 1024
HBM = pl.BlockSpec(memory_space=pltpu.HBM)
VMEM = pl.BlockSpec(memory_space=pltpu.VMEM)
SMEM = pl.BlockSpec(memory_space=pltpu.SMEM)


def dot(a, b):
    return lax.dot_general(a, b, (((1,), (0,)), ((), ())), preferred_element_type=F32)


def dot_t(a, b):
    return lax.dot_general(a, b, (((0,), (0,)), ((), ())), preferred_element_type=F32)


def start_a(acol, a_hbm, dst, rows, first, sem):
    b = a_hbm.shape[-1]
    count = dst.shape[1] // b
    for i, r in enumerate(rows):
        for k in range(a_hbm.shape[1]):
            c = jnp.clip(acol[r, k] - first, 0, count - 1)
            pltpu.make_async_copy(
                a_hbm.at[r, k], dst.at[pl.ds(i * b, b), pl.ds(pl.multiple_of(c * b, b), b)], sem
            ).start()


def place_of(rel, slots, m, r, low, high):
    coarse = slots.shape[1]
    c = jnp.clip(rel[m, r], low, high - 1)
    u = lax.div(c, coarse)
    return u * coarse + slots[u, c - u * coarse]


def start_w(rel, slots, p_hbm, w, rows, first_row, low, high, sem, first=0):
    b = p_hbm.shape[-1]
    for i, r in enumerate(rows):
        for m in range(p_hbm.shape[1]):
            q = place_of(rel, slots, m, r, low, high) - first
            pltpu.make_async_copy(
                p_hbm.at[i, m],
                w.at[pl.ds((r - first_row) * b, b), pl.ds(pl.multiple_of(q * b, b), b)],
                sem,
            ).start()


def wait_all(ref, sem):
    pltpu.make_async_copy(ref, ref, sem).wait()


def clear(ref):
    ref[...] = jnp.zeros(ref.shape, ref.dtype)


def is_even():
    return lax.rem(lax.axis_index("slab"), 2) == 0


def halo_kernel(p_hbm, pair_hbm, cross_hbm, pair, cross, s_i, s_o):
    g = GHOST
    last = p_hbm.shape[0] - g
    even = is_even()
    sides = ((jnp.where(even, 0, last), cross, cross_hbm), (jnp.where(even, last, 0), pair, pair_hbm))
    moves = []
    for i, (row, here, dst) in enumerate(sides):
        for r in range(g):
            at = i * g + r
            into = pltpu.make_async_copy(p_hbm.at[row + r], here.at[r], s_i.at[at])
            into.start()
            moves.append((into, pltpu.make_async_copy(here.at[r], dst.at[r], s_o.at[at])))
    for into, out in moves:
        into.wait()
        out.start()
    for _, out in moves:
        out.wait()


def first_kernel(
    acol, rel, slots, a_hbm, p_hbm, ghost_l, ghost_h, corner_l, corner_h, own_l, own_h, h0_hbm, l2_hbm, far_hbm,
    a_l, a_h, w, h0_v, l2_v, far, s_p, s_m, s_h, s_l, s_o,
):
    e = far.shape[0]
    g = GHOST
    one, two = slice(0, e), slice(e, 2 * e)
    outs = []

    def send(src, dst):
        outs.append(pltpu.make_async_copy(src, dst, s_o.at[len(outs)]))
        outs[-1].start()

    clear(w.at[0:e, 0 : 2 * e])
    start_w(rel, slots, p_hbm.at[0:g], w, range(g, 2 * g), g, 0, 2 * g, s_p)
    clear(w.at[2 * e : 3 * e, e : 3 * e])
    start_w(rel, slots, p_hbm.at[2 * g : 3 * g], w, range(3 * g, 4 * g), g, g, 3 * g, s_p)
    clear(a_h)
    start_a(acol, a_hbm, a_h, range(2 * g, 3 * g), g, s_h)
    clear(a_l)
    start_a(acol, a_hbm, a_l, range(0, g), 0, s_l)
    start_w(rel, slots, p_hbm.at[g : 2 * g], w, range(2 * g, 3 * g), g, g, 2 * g, s_m)
    wait_all(p_hbm.at[0 : 2 * g], s_p)
    wait_all(a_hbm.at[0:g], s_h)
    low = w[0:e, 0:e]
    high = w[2 * e : 3 * e, 2 * e : 3 * e]
    h0_v[...] = dot(a_h[:, 0:e], low).astype(BF16)
    send(h0_v, h0_hbm)
    far[:, one] = dot_t(high, h0_v[...]).astype(BF16)
    send(far.at[:, one], far_hbm.at[:, one])
    wait_all(a_hbm.at[0:g], s_l)
    l2_v[...] = dot(a_l[:, 3 * e : 4 * e], high).astype(BF16)
    send(l2_v, l2_hbm)
    far[:, two] = dot_t(low, l2_v[...]).astype(BF16)
    send(far.at[:, two], far_hbm.at[:, two])
    corner_l[...] = low
    corner_h[...] = high
    ghost_l[...] = a_l[:, 0:e]
    ghost_h[...] = a_h[:, 3 * e : 4 * e]
    own_l[:, one] = dot(a_l[:, e : 2 * e], low)
    own_h[:, two] = dot(a_h[:, 2 * e : 3 * e], high)
    wait_all(p_hbm.at[0:g], s_m)
    own_l[:, two] = dot(a_l[:, e : 4 * e], w[:, two])
    own_h[:, one] = dot(a_h[:, 0 : 3 * e], w[:, two])
    for out in outs:
        out.wait()


def second_kernel(
    rel, slots, ghost_l, ghost_h, low, high, own_l, own_h, pair, cross, l_hbm, h_hbm, pair_hbm, cross_hbm,
    w_b, w_a, l_v, h_v, up, down, s_b, s_u, s_o,
):
    e = up.shape[0]
    g = GHOST
    one, two = slice(0, e), slice(e, 2 * e)
    even = is_even()
    outs = []

    def ghosts(below, above):
        start_w(rel, slots, below, w_b, range(0, g), 0, 0, 2 * g, s_b)
        start_w(rel, slots, above, w_a, range(4 * g, 5 * g), 4 * g, g, 3 * g, s_u, g)

    def send(src, dst):
        outs.append(pltpu.make_async_copy(src, dst, s_o.at[len(outs)]))
        outs[-1].start()

    def send_to(src, if_even, if_odd):
        sem = s_o.at[len(outs)]
        outs.append(pltpu.make_async_copy(src, if_even, sem))

        @pl.when(even)
        def _():
            pltpu.make_async_copy(src, if_even, sem).start()

        @pl.when(jnp.logical_not(even))
        def _():
            pltpu.make_async_copy(src, if_odd, sem).start()

    clear(w_b)
    clear(w_a)

    @pl.when(even)
    def _():
        ghosts(cross, pair)

    @pl.when(jnp.logical_not(even))
    def _():
        ghosts(pair, cross)

    wait_all(pair, s_b)
    l_v[...] = (own_l[...] + dot(ghost_l[...], w_b[...])).astype(BF16)
    send(l_v, l_hbm)
    down[...] = dot_t(low[...], l_v[...]).astype(BF16)
    send_to(down, cross_hbm, pair_hbm)
    wait_all(cross, s_u)
    h_v[:, one] = (own_h[:, one] + dot(ghost_h[...], w_a[:, one])).astype(BF16)
    up[:, one] = dot_t(high[...], h_v[:, one]).astype(BF16)
    send_to(up.at[:, one], pair_hbm.at[:, one], cross_hbm.at[:, one])
    h_v[:, two] = (own_h[:, two] + dot(ghost_h[...], w_a[:, two])).astype(BF16)
    send(h_v, h_hbm)
    up[:, two] = dot_t(high[...], h_v[:, two]).astype(BF16)
    send_to(up.at[:, two], pair_hbm.at[:, two], cross_hbm.at[:, two])
    for out in outs:
        out.wait()


def third_kernel(
    acol, rel, slots, a_hbm, p_hbm, l_hbm, h_hbm, l2_hbm, h0_hbm, middle, a_m, ap_l, ap_m, ap_h, w, s_p, s_m, s_a
):
    e = a_m.shape[0]
    g = GHOST
    clear(w.at[0:e, 0 : 2 * e])
    start_w(rel, slots, p_hbm.at[0:g], w, range(g, 2 * g), g, 0, 2 * g, s_p)
    clear(w.at[2 * e : 3 * e, e : 3 * e])
    start_w(rel, slots, p_hbm.at[2 * g : 3 * g], w, range(3 * g, 4 * g), g, g, 3 * g, s_p)
    start_w(rel, slots, p_hbm.at[g : 2 * g], w, range(2 * g, 3 * g), g, g, 2 * g, s_p)
    clear(a_m)
    start_a(acol, a_hbm, a_m, range(g, 2 * g), g, s_m)
    moves = [
        pltpu.make_async_copy(src, dst, s_a.at[i])
        for i, (src, dst) in enumerate(
            (
                (l_hbm, ap_l.at[:, 0 : 2 * e]),
                (l2_hbm, ap_l.at[:, 2 * e : 3 * e]),
                (h0_hbm, ap_h.at[:, 0:e]),
                (h_hbm, ap_h.at[:, e : 3 * e]),
            )
        )
    ]
    for move in moves:
        move.start()
    wait_all(p_hbm, s_p)
    wait_all(a_hbm.at[g : 2 * g], s_m)
    ap_m[:, 0:e] = dot(a_m[:, 0:e], w[0:e, 0:e]).astype(BF16)
    ap_m[:, e : 2 * e] = dot(a_m[...], w[:, e : 2 * e]).astype(BF16)
    ap_m[:, 2 * e : 3 * e] = dot(a_m[:, 2 * e : 3 * e], w[2 * e : 3 * e, 2 * e : 3 * e]).astype(BF16)
    for move in moves:
        move.wait()
    w_l = w[0:e, e : 2 * e]
    w_m = w[e : 2 * e, e : 2 * e]
    w_h = w[2 * e : 3 * e, e : 2 * e]
    for c in range(3):
        at = slice(c * e, (c + 1) * e)
        middle[:, at] = dot_t(w_l, ap_l[:, at]) + dot_t(w_m, ap_m[:, at]) + dot_t(w_h, ap_h[:, at])


def fourth_kernel(middle, pair, cross, near_hbm, near, s_o):
    e = near.shape[0]
    one, two, three = (slice(c * e, (c + 1) * e) for c in range(3))
    even = is_even()

    def send(i, at):
        return pltpu.make_async_copy(near.at[:, at], near_hbm.at[:, at], s_o.at[i])

    def join(below, above):
        near[:, one] = (middle[:, one] + below[:, one].astype(F32)).astype(BF16)
        send(0, one).start()
        near[:, two] = (middle[:, two] + below[:, two].astype(F32) + above[:, one].astype(F32)).astype(BF16)
        send(1, two).start()
        near[:, three] = (middle[:, three] + above[:, two].astype(F32)).astype(BF16)
        send(2, three).start()

    @pl.when(even)
    def _():
        join(cross, pair)

    @pl.when(jnp.logical_not(even))
    def _():
        join(pair, cross)

    for i, at in enumerate((one, two, three)):
        send(i, at).wait()


def summed_kernel(far, low, high):
    e = low.shape[1]
    low[...] = sum(far[q, :, 0:e].astype(F32) for q in range(far.shape[0]))
    high[...] = sum(far[q, :, e : 2 * e].astype(F32) for q in range(far.shape[0]))


def run(body, ins, in_specs, outs, out_specs, scratch, flops):
    return pl.pallas_call(
        body,
        in_specs=in_specs,
        out_specs=out_specs,
        out_shape=outs,
        scratch_shapes=scratch,
        compiler_params=pltpu.CompilerParams(vmem_limit_bytes=VMEM_LIMIT),
        cost_estimate=pl.CostEstimate(flops=flops, transcendentals=0, bytes_accessed=8 * 1024 * 1024),
    )(*ins)


def swapped(shard, first):
    count = lax.axis_size("slab")
    pairs = [(i, i + 1) for i in range(first, count - 1, 2)]
    return lax.ppermute(shard, "slab", pairs + [(j, i) for i, j in pairs])


def passed_along(shard, by):
    count = lax.axis_size("slab")
    pairs = [(i, i + by) for i in range(count) if 0 <= i + by < count]
    return lax.ppermute(shard, "slab", pairs)


def window_cols(p_cols, coarse_slot, rows_here):
    coarse = coarse_slot.shape[1]
    slab = lax.axis_index("slab")
    column = lax.axis_index("plane")
    turned = jnp.transpose(p_cols, (0, 2, 1))
    mine = lax.dynamic_slice_in_dim(turned, column, 1, 0)[0]
    mine = jnp.pad(mine, ((0, 0), (GHOST, GHOST)))
    near = lax.dynamic_slice_in_dim(mine, slab * rows_here, rows_here + 2 * GHOST, 1)
    slots = jnp.pad(coarse_slot, ((1, 1), (0, 0)))
    return near - (slab - 1) * coarse, lax.dynamic_slice_in_dim(slots, slab, 3, 0)


def steps(a_blocks, a_cols, p_blocks, p_cols, coarse_slot):
    rows_here, b = a_blocks.shape[1], a_blocks.shape[3]
    coarse = coarse_slot.shape[1]
    e = coarse * b
    slab = lax.axis_index("slab")
    a, p = a_blocks[0], p_blocks[0]
    a = pltpu.with_memory_space_constraint(a, pltpu.HBM)
    p_here = pltpu.with_memory_space_constraint(p, pltpu.HBM)
    part = pltpu.HBM((GHOST, *p.shape[1:]), BF16)
    pair, cross = run(
        halo_kernel,
        (p_here,),
        [HBM],
        (part, part),
        (HBM, HBM),
        [pltpu.VMEM(part.shape, BF16)] * 2 + [pltpu.SemaphoreType.DMA((2 * GHOST,))] * 2,
        0,
    )
    cross = swapped(cross, 1)
    pair = swapped(pair, 0)
    rel, slots = window_cols(p_cols, coarse_slot, rows_here)
    acol = a_cols[0] - (slab * rows_here - GHOST)
    unit = 2 * e * e * b

    def shape(rows, cols, dtype=BF16, space=pltpu.VMEM):
        return space((rows * e, cols * e), dtype)

    def far_shape(rows, cols):
        return shape(rows, cols, BF16, pltpu.HBM)

    a = pltpu.with_memory_space_constraint(a, pltpu.HBM)
    p_here = pltpu.with_memory_space_constraint(p, pltpu.HBM)

    def scratch(rows, cols):
        return pltpu.VMEM((rows * e, cols * e), BF16)

    dma = pltpu.SemaphoreType.DMA(())
    *kept, ap_h0, ap_l2, far = run(
        first_kernel,
        (acol, rel, slots, a, p_here),
        [SMEM, SMEM, SMEM, HBM, HBM],
        (shape(1, 1),) * 4 + (shape(1, 2, F32),) * 2 + (far_shape(1, 1), far_shape(1, 1), far_shape(1, 2)),
        (VMEM,) * 6 + (HBM,) * 3,
        [scratch(1, 4), scratch(1, 4), scratch(3, 3), scratch(1, 1), scratch(1, 1), scratch(1, 2)]
        + [dma] * 4
        + [pltpu.SemaphoreType.DMA((4,))],
        48 * unit,
    )
    far = lax.all_to_all(far.reshape(coarse, 1, b, 2 * e), "plane", 0, 0, tiled=True)
    pair, cross = (pltpu.with_memory_space_constraint(x, pltpu.VMEM) for x in (pair, cross))
    ap_l, ap_h, pair, cross = run(
        second_kernel,
        (rel, slots, *kept, pair, cross),
        [SMEM, SMEM] + [VMEM] * 8,
        (far_shape(1, 2),) * 4,
        (HBM,) * 4,
        [scratch(1, 2)] * 6 + [dma, dma, pltpu.SemaphoreType.DMA((5,))],
        32 * unit,
    )
    cross = swapped(cross, 1)
    pair = swapped(pair, 0)
    kept = tuple(pltpu.with_memory_space_constraint(x, pltpu.HBM) for x in (ap_l, ap_h, ap_l2, ap_h0))
    middle = run(
        third_kernel,
        (acol, rel, slots, a, p_here) + kept,
        [SMEM, SMEM, SMEM] + [HBM] * 6,
        shape(1, 3, F32),
        VMEM,
        [scratch(1, 3)] * 4 + [scratch(3, 3), dma, dma, pltpu.SemaphoreType.DMA((4,))],
        56 * unit,
    )
    near = run(
        fourth_kernel,
        (middle, pair, cross),
        [VMEM] * 3,
        far_shape(1, 3),
        HBM,
        [scratch(1, 3), pltpu.SemaphoreType.DMA((3,))],
        e * 3 * e,
    )
    near = near.reshape(coarse, 1, b, 3 * e)
    near = lax.all_to_all(near, "plane", 0, 0, tiled=True)
    one = pltpu.VMEM((b, e), F32)
    low, high = run(summed_kernel, (far.reshape(coarse, b, 2 * e),), [VMEM], (one, one), (VMEM, VMEM), [], b * e * 8)
    far_low = passed_along(low, 1)
    far_high = passed_along(high, -1)
    near = jnp.sum(near.astype(F32), axis=0)
    return jnp.concatenate([far_low[None], near, far_high[None]], axis=2)[None]


def solution(mesh):
    return jax.shard_map(
        steps,
        mesh=mesh,
        in_specs=(
            P("plane", "slab", None, None, None),
            P("plane", "slab", None),
            P("plane", "slab", None, None, None),
            P(),
            P(),
        ),
        out_specs=P("plane", "slab", None, None),
        check_vma=False,
    )
```

```python
import jax
import jax.numpy as jnp
from jax import lax
from jax.experimental import pallas as pl
from jax.experimental.pallas import tpu as pltpu
from jax.sharding import PartitionSpec as P


GHOST = 4
F32 = jnp.float32
BF16 = jnp.bfloat16
VMEM_LIMIT = 20 * 1024 * 1024
HBM = pl.BlockSpec(memory_space=pltpu.HBM)
VMEM = pl.BlockSpec(memory_space=pltpu.VMEM)
SMEM = pl.BlockSpec(memory_space=pltpu.SMEM)


def dot(a, b):
    return lax.dot_general(a, b, (((1,), (0,)), ((), ())), preferred_element_type=F32)


def dot_t(a, b):
    return lax.dot_general(a, b, (((0,), (0,)), ((), ())), preferred_element_type=F32)


def start_a(acol, a_hbm, dst, rows, first, sem):
    b = a_hbm.shape[-1]
    count = dst.shape[1] // b
    for i, r in enumerate(rows):
        for k in range(a_hbm.shape[1]):
            c = jnp.clip(acol[r, k] - first, 0, count - 1)
            pltpu.make_async_copy(
                a_hbm.at[r, k], dst.at[pl.ds(i * b, b), pl.ds(pl.multiple_of(c * b, b), b)], sem
            ).start()


def place_of(rel, slots, m, r, low, high):
    coarse = slots.shape[1]
    c = jnp.clip(rel[m, r], low, high - 1)
    u = lax.div(c, coarse)
    return u * coarse + slots[u, c - u * coarse]


def start_w(rel, slots, p_hbm, w, rows, first_row, low, high, sem, first=0):
    b = p_hbm.shape[-1]
    for i, r in enumerate(rows):
        for m in range(p_hbm.shape[1]):
            q = place_of(rel, slots, m, r, low, high) - first
            pltpu.make_async_copy(
                p_hbm.at[i, m],
                w.at[pl.ds((r - first_row) * b, b), pl.ds(pl.multiple_of(q * b, b), b)],
                sem,
            ).start()


def wait_all(ref, sem):
    pltpu.make_async_copy(ref, ref, sem).wait()


def clear(ref):
    ref[...] = jnp.zeros(ref.shape, ref.dtype)


def is_even():
    return lax.rem(lax.axis_index("slab"), 2) == 0


def halo_kernel(p_hbm, pair, cross, sems):
    g = GHOST
    last = p_hbm.shape[0] - g
    even = is_even()
    sides = ((jnp.where(even, 0, last), cross), (jnp.where(even, last, 0), pair))
    moves = [pltpu.make_async_copy(p_hbm.at[pl.ds(row, g)], dst, sems.at[i]) for i, (row, dst) in enumerate(sides)]
    for move in moves:
        move.start()
    for move in moves:
        move.wait()


def first_kernel(
    acol, rel, slots, a_hbm, p_hbm, ghost_l, ghost_h, corner_l, corner_h, own_l, own_h, h0_hbm, l2_hbm, far_hbm,
    a_l, a_h, w, h0_v, l2_v, far, s_p, s_m, s_h, s_l, s_o,
):
    e = far.shape[0]
    g = GHOST
    one, two = slice(0, e), slice(e, 2 * e)
    outs = []

    def send(src, dst):
        outs.append(pltpu.make_async_copy(src, dst, s_o.at[len(outs)]))
        outs[-1].start()

    clear(w.at[0:e, 0 : 2 * e])
    start_w(rel, slots, p_hbm.at[0:g], w, range(g, 2 * g), g, 0, 2 * g, s_p)
    clear(w.at[2 * e : 3 * e, e : 3 * e])
    start_w(rel, slots, p_hbm.at[2 * g : 3 * g], w, range(3 * g, 4 * g), g, g, 3 * g, s_p)
    clear(a_h)
    start_a(acol, a_hbm, a_h, range(2 * g, 3 * g), g, s_h)
    clear(a_l)
    start_a(acol, a_hbm, a_l, range(0, g), 0, s_l)
    start_w(rel, slots, p_hbm.at[g : 2 * g], w, range(2 * g, 3 * g), g, g, 2 * g, s_m)
    wait_all(p_hbm.at[0 : 2 * g], s_p)
    wait_all(a_hbm.at[0:g], s_h)
    low = w[0:e, 0:e]
    high = w[2 * e : 3 * e, 2 * e : 3 * e]
    h0_v[...] = dot(a_h[:, 0:e], low).astype(BF16)
    send(h0_v, h0_hbm)
    far[:, one] = dot_t(high, h0_v[...]).astype(BF16)
    send(far.at[:, one], far_hbm.at[:, one])
    wait_all(a_hbm.at[0:g], s_l)
    l2_v[...] = dot(a_l[:, 3 * e : 4 * e], high).astype(BF16)
    send(l2_v, l2_hbm)
    far[:, two] = dot_t(low, l2_v[...]).astype(BF16)
    send(far.at[:, two], far_hbm.at[:, two])
    corner_l[...] = low
    corner_h[...] = high
    ghost_l[...] = a_l[:, 0:e]
    ghost_h[...] = a_h[:, 3 * e : 4 * e]
    own_l[:, one] = dot(a_l[:, e : 2 * e], low)
    own_h[:, two] = dot(a_h[:, 2 * e : 3 * e], high)
    wait_all(p_hbm.at[0:g], s_m)
    own_l[:, two] = dot(a_l[:, e : 4 * e], w[:, two])
    own_h[:, one] = dot(a_h[:, 0 : 3 * e], w[:, two])
    for out in outs:
        out.wait()


def second_kernel(
    rel, slots, ghost_l, ghost_h, low, high, own_l, own_h, pair, cross, l_hbm, h_hbm, pair_hbm, cross_hbm,
    w_b, w_a, l_v, h_v, up, down, s_b, s_u, s_o,
):
    e = up.shape[0]
    g = GHOST
    one, two = slice(0, e), slice(e, 2 * e)
    even = is_even()
    outs = []

    def ghost_below(below):
        start_w(rel, slots, below, w_b, range(0, g), 0, 0, 2 * g, s_b)

    def ghost_above(above):
        start_w(rel, slots, above, w_a, range(4 * g, 5 * g), 4 * g, g, 3 * g, s_u, g)

    def by_parity(start, if_even, if_odd):
        @pl.when(even)
        def _():
            start(if_even)

        @pl.when(jnp.logical_not(even))
        def _():
            start(if_odd)

    def send(src, dst):
        outs.append(pltpu.make_async_copy(src, dst, s_o.at[len(outs)]))
        outs[-1].start()

    def send_to(src, if_even, if_odd):
        sem = s_o.at[len(outs)]
        outs.append(pltpu.make_async_copy(src, if_even, sem))

        @pl.when(even)
        def _():
            pltpu.make_async_copy(src, if_even, sem).start()

        @pl.when(jnp.logical_not(even))
        def _():
            pltpu.make_async_copy(src, if_odd, sem).start()

    clear(w_b)
    by_parity(ghost_below, cross, pair)
    clear(w_a)
    by_parity(ghost_above, pair, cross)
    wait_all(pair, s_b)
    l_v[...] = (own_l[...] + dot(ghost_l[...], w_b[...])).astype(BF16)
    send(l_v, l_hbm)
    down[...] = dot_t(low[...], l_v[...]).astype(BF16)
    send_to(down, cross_hbm, pair_hbm)
    wait_all(cross, s_u)
    h_v[:, one] = (own_h[:, one] + dot(ghost_h[...], w_a[:, one])).astype(BF16)
    up[:, one] = dot_t(high[...], h_v[:, one]).astype(BF16)
    send_to(up.at[:, one], pair_hbm.at[:, one], cross_hbm.at[:, one])
    h_v[:, two] = (own_h[:, two] + dot(ghost_h[...], w_a[:, two])).astype(BF16)
    send(h_v, h_hbm)
    for at in (slice(e, e + e // 2), slice(e + e // 2, 2 * e)):
        up[:, at] = dot_t(high[...], h_v[:, at]).astype(BF16)
        send_to(up.at[:, at], pair_hbm.at[:, at], cross_hbm.at[:, at])
    for out in outs:
        out.wait()


def third_kernel(
    acol, rel, slots, a_hbm, p_hbm, l_hbm, h_hbm, l2_hbm, h0_hbm, middle, a_m, ap_l, ap_m, ap_h, w, s_p, s_m, s_a
):
    e = a_m.shape[0]
    g = GHOST
    clear(w.at[0:e, 0 : 2 * e])
    start_w(rel, slots, p_hbm.at[0:g], w, range(g, 2 * g), g, 0, 2 * g, s_p)
    clear(w.at[2 * e : 3 * e, e : 3 * e])
    start_w(rel, slots, p_hbm.at[2 * g : 3 * g], w, range(3 * g, 4 * g), g, g, 3 * g, s_p)
    start_w(rel, slots, p_hbm.at[g : 2 * g], w, range(2 * g, 3 * g), g, g, 2 * g, s_p)
    clear(a_m)
    start_a(acol, a_hbm, a_m, range(g, 2 * g), g, s_m)
    moves = [
        pltpu.make_async_copy(src, dst, s_a.at[i])
        for i, (src, dst) in enumerate(
            (
                (l_hbm, ap_l.at[:, 0 : 2 * e]),
                (l2_hbm, ap_l.at[:, 2 * e : 3 * e]),
                (h0_hbm, ap_h.at[:, 0:e]),
                (h_hbm, ap_h.at[:, e : 3 * e]),
            )
        )
    ]
    for move in moves:
        move.start()
    wait_all(p_hbm, s_p)
    wait_all(a_hbm.at[g : 2 * g], s_m)
    ap_m[:, 0:e] = dot(a_m[:, 0:e], w[0:e, 0:e]).astype(BF16)
    ap_m[:, e : 2 * e] = dot(a_m[...], w[:, e : 2 * e]).astype(BF16)
    ap_m[:, 2 * e : 3 * e] = dot(a_m[:, 2 * e : 3 * e], w[2 * e : 3 * e, 2 * e : 3 * e]).astype(BF16)
    for move in moves:
        move.wait()
    w_l = w[0:e, e : 2 * e]
    w_m = w[e : 2 * e, e : 2 * e]
    w_h = w[2 * e : 3 * e, e : 2 * e]
    for c in range(3):
        at = slice(c * e, (c + 1) * e)
        middle[:, at] = dot_t(w_l, ap_l[:, at]) + dot_t(w_m, ap_m[:, at]) + dot_t(w_h, ap_h[:, at])


def fourth_kernel(middle, pair, cross, near_hbm, near, s_o):
    e = near.shape[0]
    one, two, three = (slice(c * e, (c + 1) * e) for c in range(3))
    even = is_even()

    def send(i, at):
        return pltpu.make_async_copy(near.at[:, at], near_hbm.at[:, at], s_o.at[i])

    def join(below, above):
        near[:, one] = (middle[:, one] + below[:, one].astype(F32)).astype(BF16)
        send(0, one).start()
        near[:, two] = (middle[:, two] + below[:, two].astype(F32) + above[:, one].astype(F32)).astype(BF16)
        send(1, two).start()
        near[:, three] = (middle[:, three] + above[:, two].astype(F32)).astype(BF16)
        send(2, three).start()

    @pl.when(even)
    def _():
        join(cross, pair)

    @pl.when(jnp.logical_not(even))
    def _():
        join(pair, cross)

    for i, at in enumerate((one, two, three)):
        send(i, at).wait()


def summed_kernel(far, low, high):
    e = low.shape[1]
    low[...] = sum(far[q, :, 0:e].astype(F32) for q in range(far.shape[0]))
    high[...] = sum(far[q, :, e : 2 * e].astype(F32) for q in range(far.shape[0]))


def run(body, ins, in_specs, outs, out_specs, scratch, flops):
    return pl.pallas_call(
        body,
        in_specs=in_specs,
        out_specs=out_specs,
        out_shape=outs,
        scratch_shapes=scratch,
        compiler_params=pltpu.CompilerParams(vmem_limit_bytes=VMEM_LIMIT),
        cost_estimate=pl.CostEstimate(flops=flops, transcendentals=0, bytes_accessed=8 * 1024 * 1024),
    )(*ins)


def swapped(shard, first):
    count = lax.axis_size("slab")
    pairs = [(i, i + 1) for i in range(first, count - 1, 2)]
    return lax.ppermute(shard, "slab", pairs + [(j, i) for i, j in pairs])


def passed_along(shard, by):
    count = lax.axis_size("slab")
    pairs = [(i, i + by) for i in range(count) if 0 <= i + by < count]
    return lax.ppermute(shard, "slab", pairs)


def window_cols(p_cols, coarse_slot, rows_here):
    coarse = coarse_slot.shape[1]
    slab = lax.axis_index("slab")
    column = lax.axis_index("plane")
    turned = jnp.transpose(p_cols, (0, 2, 1))
    mine = lax.dynamic_slice_in_dim(turned, column, 1, 0)[0]
    mine = jnp.pad(mine, ((0, 0), (GHOST, GHOST)))
    near = lax.dynamic_slice_in_dim(mine, slab * rows_here, rows_here + 2 * GHOST, 1)
    slots = jnp.pad(coarse_slot, ((1, 1), (0, 0)))
    return near - (slab - 1) * coarse, lax.dynamic_slice_in_dim(slots, slab, 3, 0)


def steps(a_blocks, a_cols, p_blocks, p_cols, coarse_slot):
    rows_here, b = a_blocks.shape[1], a_blocks.shape[3]
    coarse = coarse_slot.shape[1]
    e = coarse * b
    slab = lax.axis_index("slab")
    a, p = a_blocks[0], p_blocks[0]
    a = pltpu.with_memory_space_constraint(a, pltpu.HBM)
    p_here = pltpu.with_memory_space_constraint(p, pltpu.HBM)
    part = pltpu.VMEM((GHOST, *p.shape[1:]), BF16)
    pair, cross = run(halo_kernel, (p_here,), [HBM], (part, part), (VMEM, VMEM), [pltpu.SemaphoreType.DMA((2,))], 0)
    cross = swapped(cross, 1)
    pair = swapped(pair, 0)
    rel, slots = window_cols(p_cols, coarse_slot, rows_here)
    acol = a_cols[0] - (slab * rows_here - GHOST)
    unit = 2 * e * e * b

    def shape(rows, cols, dtype=BF16, space=pltpu.VMEM):
        return space((rows * e, cols * e), dtype)

    def far_shape(rows, cols):
        return shape(rows, cols, BF16, pltpu.HBM)

    a = pltpu.with_memory_space_constraint(a, pltpu.HBM)
    p_here = pltpu.with_memory_space_constraint(p, pltpu.HBM)

    def scratch(rows, cols):
        return pltpu.VMEM((rows * e, cols * e), BF16)

    dma = pltpu.SemaphoreType.DMA(())
    *kept, ap_h0, ap_l2, far = run(
        first_kernel,
        (acol, rel, slots, a, p_here),
        [SMEM, SMEM, SMEM, HBM, HBM],
        (shape(1, 1),) * 4 + (shape(1, 2, F32),) * 2 + (far_shape(1, 1), far_shape(1, 1), far_shape(1, 2)),
        (VMEM,) * 6 + (HBM,) * 3,
        [scratch(1, 4), scratch(1, 4), scratch(3, 3), scratch(1, 1), scratch(1, 1), scratch(1, 2)]
        + [dma] * 4
        + [pltpu.SemaphoreType.DMA((4,))],
        48 * unit,
    )
    far = lax.all_to_all(far.reshape(coarse, 1, b, 2 * e), "plane", 0, 0, tiled=True)
    pair, cross = (pltpu.with_memory_space_constraint(x, pltpu.VMEM) for x in (pair, cross))
    ap_l, ap_h, pair, cross = run(
        second_kernel,
        (rel, slots, *kept, pair, cross),
        [SMEM, SMEM] + [VMEM] * 8,
        (far_shape(1, 2),) * 4,
        (HBM,) * 4,
        [scratch(1, 2)] * 6 + [dma, dma, pltpu.SemaphoreType.DMA((6,))],
        32 * unit,
    )
    cross = swapped(cross, 1)
    pair = swapped(pair, 0)
    kept = tuple(pltpu.with_memory_space_constraint(x, pltpu.HBM) for x in (ap_l, ap_h, ap_l2, ap_h0))
    middle = run(
        third_kernel,
        (acol, rel, slots, a, p_here) + kept,
        [SMEM, SMEM, SMEM] + [HBM] * 6,
        shape(1, 3, F32),
        VMEM,
        [scratch(1, 3)] * 4 + [scratch(3, 3), dma, dma, pltpu.SemaphoreType.DMA((4,))],
        56 * unit,
    )
    near = run(
        fourth_kernel,
        (middle, pair, cross),
        [VMEM] * 3,
        far_shape(1, 3),
        HBM,
        [scratch(1, 3), pltpu.SemaphoreType.DMA((3,))],
        e * 3 * e,
    )
    near = near.reshape(coarse, 1, b, 3 * e)
    near = lax.all_to_all(near, "plane", 0, 0, tiled=True)
    one = pltpu.VMEM((b, e), F32)
    low, high = run(summed_kernel, (far.reshape(coarse, b, 2 * e),), [VMEM], (one, one), (VMEM, VMEM), [], b * e * 8)
    far_low = passed_along(low, 1)
    far_high = passed_along(high, -1)
    near = jnp.sum(near.astype(F32), axis=0)
    return jnp.concatenate([far_low[None], near, far_high[None]], axis=2)[None]


def solution(mesh):
    return jax.shard_map(
        steps,
        mesh=mesh,
        in_specs=(
            P("plane", "slab", None, None, None),
            P("plane", "slab", None),
            P("plane", "slab", None, None, None),
            P(),
            P(),
        ),
        out_specs=P("plane", "slab", None, None),
        check_vma=False,
    )
```

```python
import jax
import jax.numpy as jnp
from jax import lax
from jax.experimental import pallas as pl
from jax.experimental.pallas import tpu as pltpu
from jax.sharding import PartitionSpec as P


GHOST = 4
OTHERS = (2, 1, 3)
F32 = jnp.float32
BF16 = jnp.bfloat16
VMEM_LIMIT = 20 * 1024 * 1024
HBM = pl.BlockSpec(memory_space=pltpu.HBM)
VMEM = pl.BlockSpec(memory_space=pltpu.VMEM)
SMEM = pl.BlockSpec(memory_space=pltpu.SMEM)


def dot(a, b):
    return lax.dot_general(a, b, (((1,), (0,)), ((), ())), preferred_element_type=F32)


def dot_t(a, b):
    return lax.dot_general(a, b, (((0,), (0,)), ((), ())), preferred_element_type=F32)


def start_a(acol, a_hbm, dst, rows, first, sem):
    b = a_hbm.shape[-1]
    count = dst.shape[1] // b
    for i, r in enumerate(rows):
        for k in range(a_hbm.shape[1]):
            c = jnp.clip(acol[r, k] - first, 0, count - 1)
            pltpu.make_async_copy(
                a_hbm.at[r, k], dst.at[pl.ds(i * b, b), pl.ds(pl.multiple_of(c * b, b), b)], sem
            ).start()


def place_of(rel, slots, m, r, low, high):
    coarse = slots.shape[1]
    c = jnp.clip(rel[m, r], low, high - 1)
    u = lax.div(c, coarse)
    return u * coarse + slots[u, c - u * coarse]


def start_w(rel, slots, p_hbm, w, rows, first_row, low, high, sem, first=0):
    b = p_hbm.shape[-1]
    for i, r in enumerate(rows):
        for m in range(p_hbm.shape[1]):
            q = place_of(rel, slots, m, r, low, high) - first
            pltpu.make_async_copy(
                p_hbm.at[i, m],
                w.at[pl.ds((r - first_row) * b, b), pl.ds(pl.multiple_of(q * b, b), b)],
                sem,
            ).start()


def wait_all(ref, sem):
    pltpu.make_async_copy(ref, ref, sem).wait()


def clear(ref):
    ref[...] = jnp.zeros(ref.shape, ref.dtype)


def is_even():
    return lax.rem(lax.axis_index("slab"), 2) == 0


def halo_kernel(p_hbm, pair, cross, sems):
    g = GHOST
    last = p_hbm.shape[0] - g
    even = is_even()
    sides = ((jnp.where(even, 0, last), cross), (jnp.where(even, last, 0), pair))
    moves = [pltpu.make_async_copy(p_hbm.at[pl.ds(row, g)], dst, sems.at[i]) for i, (row, dst) in enumerate(sides)]
    for move in moves:
        move.start()
    for move in moves:
        move.wait()


def first_kernel(
    acol, rel, slots, a_hbm, p_hbm, ghost_l, ghost_h, corner_l, corner_h, own_l, own_h, h0_hbm, l2_hbm, far_hbm,
    a_l, a_h, w, h0_v, l2_v, far, s_p, s_m, s_h, s_l, s_o,
):
    e = far.shape[0]
    g = GHOST
    one, two = slice(0, e), slice(e, 2 * e)
    outs = []

    def send(src, dst):
        outs.append(pltpu.make_async_copy(src, dst, s_o.at[len(outs)]))
        outs[-1].start()

    clear(w.at[0:e, 0 : 2 * e])
    start_w(rel, slots, p_hbm.at[0:g], w, range(g, 2 * g), g, 0, 2 * g, s_p)
    clear(w.at[2 * e : 3 * e, e : 3 * e])
    start_w(rel, slots, p_hbm.at[2 * g : 3 * g], w, range(3 * g, 4 * g), g, g, 3 * g, s_p)
    clear(a_h)
    start_a(acol, a_hbm, a_h, range(2 * g, 3 * g), g, s_h)
    clear(a_l)
    start_a(acol, a_hbm, a_l, range(0, g), 0, s_l)
    start_w(rel, slots, p_hbm.at[g : 2 * g], w, range(2 * g, 3 * g), g, g, 2 * g, s_m)
    wait_all(p_hbm.at[0 : 2 * g], s_p)
    wait_all(a_hbm.at[0:g], s_h)
    low = w[0:e, 0:e]
    high = w[2 * e : 3 * e, 2 * e : 3 * e]
    h0_v[...] = dot(a_h[:, 0:e], low).astype(BF16)
    send(h0_v, h0_hbm)
    far[:, one] = dot_t(high, h0_v[...]).astype(BF16)
    send(far.at[:, one], far_hbm.at[:, one])
    wait_all(a_hbm.at[0:g], s_l)
    l2_v[...] = dot(a_l[:, 3 * e : 4 * e], high).astype(BF16)
    send(l2_v, l2_hbm)
    far[:, two] = dot_t(low, l2_v[...]).astype(BF16)
    send(far.at[:, two], far_hbm.at[:, two])
    corner_l[...] = low
    corner_h[...] = high
    ghost_l[...] = a_l[:, 0:e]
    ghost_h[...] = a_h[:, 3 * e : 4 * e]
    own_l[:, one] = dot(a_l[:, e : 2 * e], low)
    own_h[:, two] = dot(a_h[:, 2 * e : 3 * e], high)
    wait_all(p_hbm.at[0:g], s_m)
    own_l[:, two] = dot(a_l[:, e : 4 * e], w[:, two])
    own_h[:, one] = dot(a_h[:, 0 : 3 * e], w[:, two])
    for out in outs:
        out.wait()


def second_kernel(
    rel, slots, ghost_l, ghost_h, low, high, own_l, own_h, pair, cross, l_hbm, h_hbm, pair_hbm, cross_hbm,
    w_b, w_a, l_v, h_v, up, down, s_b, s_u, s_o,
):
    e = up.shape[0]
    g = GHOST
    one, two = slice(0, e), slice(e, 2 * e)
    even = is_even()
    outs = []

    def ghost_below(below):
        start_w(rel, slots, below, w_b, range(0, g), 0, 0, 2 * g, s_b)

    def ghost_above(above):
        start_w(rel, slots, above, w_a, range(4 * g, 5 * g), 4 * g, g, 3 * g, s_u, g)

    def by_parity(start, if_even, if_odd):
        @pl.when(even)
        def _():
            start(if_even)

        @pl.when(jnp.logical_not(even))
        def _():
            start(if_odd)

    def send(src, dst):
        outs.append(pltpu.make_async_copy(src, dst, s_o.at[len(outs)]))
        outs[-1].start()

    def send_to(src, if_even, if_odd):
        sem = s_o.at[len(outs)]
        outs.append(pltpu.make_async_copy(src, if_even, sem))

        @pl.when(even)
        def _():
            pltpu.make_async_copy(src, if_even, sem).start()

        @pl.when(jnp.logical_not(even))
        def _():
            pltpu.make_async_copy(src, if_odd, sem).start()

    clear(w_b)
    by_parity(ghost_below, cross, pair)
    clear(w_a)
    by_parity(ghost_above, pair, cross)
    wait_all(pair, s_b)
    l_v[...] = (own_l[...] + dot(ghost_l[...], w_b[...])).astype(BF16)
    send(l_v, l_hbm)
    down[...] = dot_t(low[...], l_v[...]).astype(BF16)
    send_to(down, cross_hbm, pair_hbm)
    wait_all(cross, s_u)
    h_v[:, one] = (own_h[:, one] + dot(ghost_h[...], w_a[:, one])).astype(BF16)
    up[:, one] = dot_t(high[...], h_v[:, one]).astype(BF16)
    send_to(up.at[:, one], pair_hbm.at[:, one], cross_hbm.at[:, one])
    h_v[:, two] = (own_h[:, two] + dot(ghost_h[...], w_a[:, two])).astype(BF16)
    send(h_v, h_hbm)
    for at in (slice(e, e + e // 2), slice(e + e // 2, 2 * e)):
        up[:, at] = dot_t(high[...], h_v[:, at]).astype(BF16)
        send_to(up.at[:, at], pair_hbm.at[:, at], cross_hbm.at[:, at])
    for out in outs:
        out.wait()


def third_kernel(
    acol, rel, slots, a_hbm, p_hbm, l_hbm, h_hbm, l2_hbm, h0_hbm, middle, a_m, ap_l, ap_m, ap_h, w, s_p, s_m, s_a
):
    e = a_m.shape[0]
    g = GHOST
    clear(w.at[0:e, 0 : 2 * e])
    start_w(rel, slots, p_hbm.at[0:g], w, range(g, 2 * g), g, 0, 2 * g, s_p)
    clear(w.at[2 * e : 3 * e, e : 3 * e])
    start_w(rel, slots, p_hbm.at[2 * g : 3 * g], w, range(3 * g, 4 * g), g, g, 3 * g, s_p)
    start_w(rel, slots, p_hbm.at[g : 2 * g], w, range(2 * g, 3 * g), g, g, 2 * g, s_p)
    clear(a_m)
    start_a(acol, a_hbm, a_m, range(g, 2 * g), g, s_m)
    moves = [
        pltpu.make_async_copy(src, dst, s_a.at[i])
        for i, (src, dst) in enumerate(
            (
                (l_hbm, ap_l.at[:, 0 : 2 * e]),
                (l2_hbm, ap_l.at[:, 2 * e : 3 * e]),
                (h0_hbm, ap_h.at[:, 0:e]),
                (h_hbm, ap_h.at[:, e : 3 * e]),
            )
        )
    ]
    for move in moves:
        move.start()
    wait_all(p_hbm, s_p)
    wait_all(a_hbm.at[g : 2 * g], s_m)
    ap_m[:, 0:e] = dot(a_m[:, 0:e], w[0:e, 0:e]).astype(BF16)
    ap_m[:, e : 2 * e] = dot(a_m[...], w[:, e : 2 * e]).astype(BF16)
    ap_m[:, 2 * e : 3 * e] = dot(a_m[:, 2 * e : 3 * e], w[2 * e : 3 * e, 2 * e : 3 * e]).astype(BF16)
    for move in moves:
        move.wait()
    w_l = w[0:e, e : 2 * e]
    w_m = w[e : 2 * e, e : 2 * e]
    w_h = w[2 * e : 3 * e, e : 2 * e]
    for c in range(3):
        at = slice(c * e, (c + 1) * e)
        middle[:, at] = dot_t(w_l, ap_l[:, at]) + dot_t(w_m, ap_m[:, at]) + dot_t(w_h, ap_h[:, at])


def fourth_kernel(middle, pair, cross, own, *refs):
    count = len(refs) // 2
    outs, (*nears, s_o) = refs[:count], refs[count:]
    b = own.shape[0]
    e = pair.shape[0]
    one, two, three = (slice(c * e, (c + 1) * e) for c in range(3))
    even = is_even()
    plane = lax.axis_index("plane")

    def join(below, above):
        for d in OTHERS + (0,):
            rows = pl.ds(pl.multiple_of((plane ^ d) * b, b), b)
            to = nears[OTHERS.index(d)] if d else own
            to[:, one] = (middle[rows, one] + below[rows, one].astype(F32)).astype(to.dtype)
            total = middle[rows, two] + below[rows, two].astype(F32) + above[rows, one].astype(F32)
            to[:, two] = total.astype(to.dtype)
            to[:, three] = (middle[rows, three] + above[rows, two].astype(F32)).astype(to.dtype)
            if d:
                k = OTHERS.index(d)
                pltpu.make_async_copy(nears[k], outs[k], s_o.at[k]).start()

    @pl.when(even)
    def _():
        join(cross, pair)

    @pl.when(jnp.logical_not(even))
    def _():
        join(pair, cross)

    for k in range(count):
        pltpu.make_async_copy(nears[k], outs[k], s_o.at[k]).wait()


def summed_kernel(far, low, high):
    e = low.shape[1]
    low[...] = sum(far[q, :, 0:e].astype(F32) for q in range(far.shape[0]))
    high[...] = sum(far[q, :, e : 2 * e].astype(F32) for q in range(far.shape[0]))


def run(body, ins, in_specs, outs, out_specs, scratch, flops):
    return pl.pallas_call(
        body,
        in_specs=in_specs,
        out_specs=out_specs,
        out_shape=outs,
        scratch_shapes=scratch,
        compiler_params=pltpu.CompilerParams(vmem_limit_bytes=VMEM_LIMIT),
        cost_estimate=pl.CostEstimate(flops=flops, transcendentals=0, bytes_accessed=8 * 1024 * 1024),
    )(*ins)


def swapped(shard, first):
    count = lax.axis_size("slab")
    pairs = [(i, i + 1) for i in range(first, count - 1, 2)]
    return lax.ppermute(shard, "slab", pairs + [(j, i) for i, j in pairs])


def passed_along(shard, by):
    count = lax.axis_size("slab")
    pairs = [(i, i + by) for i in range(count) if 0 <= i + by < count]
    return lax.ppermute(shard, "slab", pairs)


def window_cols(p_cols, coarse_slot, rows_here):
    coarse = coarse_slot.shape[1]
    slab = lax.axis_index("slab")
    column = lax.axis_index("plane")
    turned = jnp.transpose(p_cols, (0, 2, 1))
    mine = lax.dynamic_slice_in_dim(turned, column, 1, 0)[0]
    mine = jnp.pad(mine, ((0, 0), (GHOST, GHOST)))
    near = lax.dynamic_slice_in_dim(mine, slab * rows_here, rows_here + 2 * GHOST, 1)
    slots = jnp.pad(coarse_slot, ((1, 1), (0, 0)))
    return near - (slab - 1) * coarse, lax.dynamic_slice_in_dim(slots, slab, 3, 0)


def steps(a_blocks, a_cols, p_blocks, p_cols, coarse_slot):
    rows_here, b = a_blocks.shape[1], a_blocks.shape[3]
    coarse = coarse_slot.shape[1]
    e = coarse * b
    slab = lax.axis_index("slab")
    a, p = a_blocks[0], p_blocks[0]
    a = pltpu.with_memory_space_constraint(a, pltpu.HBM)
    p_here = pltpu.with_memory_space_constraint(p, pltpu.HBM)
    part = pltpu.VMEM((GHOST, *p.shape[1:]), BF16)
    pair, cross = run(halo_kernel, (p_here,), [HBM], (part, part), (VMEM, VMEM), [pltpu.SemaphoreType.DMA((2,))], 0)
    cross = swapped(cross, 1)
    pair = swapped(pair, 0)
    rel, slots = window_cols(p_cols, coarse_slot, rows_here)
    acol = a_cols[0] - (slab * rows_here - GHOST)
    unit = 2 * e * e * b

    def shape(rows, cols, dtype=BF16, space=pltpu.VMEM):
        return space((rows * e, cols * e), dtype)

    def far_shape(rows, cols):
        return shape(rows, cols, BF16, pltpu.HBM)

    a = pltpu.with_memory_space_constraint(a, pltpu.HBM)
    p_here = pltpu.with_memory_space_constraint(p, pltpu.HBM)

    def scratch(rows, cols):
        return pltpu.VMEM((rows * e, cols * e), BF16)

    dma = pltpu.SemaphoreType.DMA(())
    *kept, ap_h0, ap_l2, far = run(
        first_kernel,
        (acol, rel, slots, a, p_here),
        [SMEM, SMEM, SMEM, HBM, HBM],
        (shape(1, 1),) * 4 + (shape(1, 2, F32),) * 2 + (far_shape(1, 1), far_shape(1, 1), far_shape(1, 2)),
        (VMEM,) * 6 + (HBM,) * 3,
        [scratch(1, 4), scratch(1, 4), scratch(3, 3), scratch(1, 1), scratch(1, 1), scratch(1, 2)]
        + [dma] * 4
        + [pltpu.SemaphoreType.DMA((4,))],
        48 * unit,
    )
    far = lax.all_to_all(far.reshape(coarse, 1, b, 2 * e), "plane", 0, 0, tiled=True)
    pair, cross = (pltpu.with_memory_space_constraint(x, pltpu.VMEM) for x in (pair, cross))
    ap_l, ap_h, pair, cross = run(
        second_kernel,
        (rel, slots, *kept, pair, cross),
        [SMEM, SMEM] + [VMEM] * 8,
        (far_shape(1, 2),) * 4,
        (HBM,) * 4,
        [scratch(1, 2)] * 6 + [dma, dma, pltpu.SemaphoreType.DMA((6,))],
        32 * unit,
    )
    cross = swapped(cross, 1)
    pair = swapped(pair, 0)
    kept = tuple(pltpu.with_memory_space_constraint(x, pltpu.HBM) for x in (ap_l, ap_h, ap_l2, ap_h0))
    middle = run(
        third_kernel,
        (acol, rel, slots, a, p_here) + kept,
        [SMEM, SMEM, SMEM] + [HBM] * 6,
        shape(1, 3, F32),
        VMEM,
        [scratch(1, 3)] * 4 + [scratch(3, 3), dma, dma, pltpu.SemaphoreType.DMA((4,))],
        56 * unit,
    )
    chunk = ((b, 3 * e), BF16)
    own, *nears = run(
        fourth_kernel,
        (middle, pair, cross),
        [VMEM] * 3,
        (pltpu.VMEM((b, 3 * e), F32),) + (pltpu.HBM(*chunk),) * len(OTHERS),
        (VMEM,) + (HBM,) * len(OTHERS),
        [pltpu.VMEM(*chunk)] * len(OTHERS) + [pltpu.SemaphoreType.DMA((len(OTHERS),))],
        e * 3 * e,
    )
    got = []
    for k, d in enumerate(OTHERS):
        got.append(lax.ppermute(nears[k], "plane", [(q, q ^ d) for q in range(lax.axis_size("plane"))]))
    one = pltpu.VMEM((b, e), F32)
    low, high = run(summed_kernel, (far.reshape(coarse, b, 2 * e),), [VMEM], (one, one), (VMEM, VMEM), [], b * e * 8)
    far_low = passed_along(low, 1)
    far_high = passed_along(high, -1)
    near = (own + sum(x.astype(F32) for x in got))[None]
    return jnp.concatenate([far_low[None], near, far_high[None]], axis=2)[None]


def solution(mesh):
    return jax.shard_map(
        steps,
        mesh=mesh,
        in_specs=(
            P("plane", "slab", None, None, None),
            P("plane", "slab", None),
            P("plane", "slab", None, None, None),
            P(),
            P(),
        ),
        out_specs=P("plane", "slab", None, None),
        check_vma=False,
    )
```

```python
import jax
import jax.numpy as jnp
from jax import lax
from jax.experimental import pallas as pl
from jax.experimental.pallas import tpu as pltpu
from jax.sharding import PartitionSpec as P


GHOST = 4
OTHERS = (2, 1, 3)
F32 = jnp.float32
BF16 = jnp.bfloat16
VMEM_LIMIT = 20 * 1024 * 1024
HBM = pl.BlockSpec(memory_space=pltpu.HBM)
VMEM = pl.BlockSpec(memory_space=pltpu.VMEM)
SMEM = pl.BlockSpec(memory_space=pltpu.SMEM)


def dot(a, b):
    return lax.dot_general(a, b, (((1,), (0,)), ((), ())), preferred_element_type=F32)


def dot_t(a, b):
    return lax.dot_general(a, b, (((0,), (0,)), ((), ())), preferred_element_type=F32)


def start_a(acol, a_hbm, dst, rows, first, sem):
    b = a_hbm.shape[-1]
    count = dst.shape[1] // b
    for i, r in enumerate(rows):
        for k in range(a_hbm.shape[1]):
            c = jnp.clip(acol[r, k] - first, 0, count - 1)
            pltpu.make_async_copy(
                a_hbm.at[r, k], dst.at[pl.ds(i * b, b), pl.ds(pl.multiple_of(c * b, b), b)], sem
            ).start()


def place_of(rel, slots, m, r, low, high):
    coarse = slots.shape[1]
    c = jnp.clip(rel[m, r], low, high - 1)
    u = lax.div(c, coarse)
    return u * coarse + slots[u, c - u * coarse]


def start_w(rel, slots, p_hbm, w, rows, first_row, low, high, sem, first=0):
    b = p_hbm.shape[-1]
    for i, r in enumerate(rows):
        for m in range(p_hbm.shape[1]):
            q = place_of(rel, slots, m, r, low, high) - first
            pltpu.make_async_copy(
                p_hbm.at[i, m],
                w.at[pl.ds((r - first_row) * b, b), pl.ds(pl.multiple_of(q * b, b), b)],
                sem,
            ).start()


def wait_all(ref, sem):
    pltpu.make_async_copy(ref, ref, sem).wait()


def clear(ref):
    ref[...] = jnp.zeros(ref.shape, ref.dtype)


def is_even():
    return lax.rem(lax.axis_index("slab"), 2) == 0


def halo_kernel(p_hbm, pair, cross, sems):
    g = GHOST
    last = p_hbm.shape[0] - g
    even = is_even()
    sides = ((jnp.where(even, 0, last), cross), (jnp.where(even, last, 0), pair))
    moves = [pltpu.make_async_copy(p_hbm.at[pl.ds(row, g)], dst, sems.at[i]) for i, (row, dst) in enumerate(sides)]
    for move in moves:
        move.start()
    for move in moves:
        move.wait()


def first_kernel(
    acol, rel, slots, a_hbm, p_hbm, ghost_l, ghost_h, corner_l, corner_h, own_l, own_h, h0_hbm, l2_hbm, *rest,
):
    fars, (a_l, a_h, w, h0_v, l2_v, far, s_p, s_m, s_h, s_l, s_o) = rest[:-11], rest[-11:]
    e = far.shape[0]
    b = fars[0].shape[0]
    plane = lax.axis_index("plane")
    g = GHOST
    one, two = slice(0, e), slice(e, 2 * e)
    outs = []

    def send(src, dst):
        outs.append(pltpu.make_async_copy(src, dst, s_o.at[len(outs)]))
        outs[-1].start()

    def send_far(at):
        for d, dst in zip((0,) + OTHERS, fars):
            send(far.at[pl.ds(pl.multiple_of((plane ^ d) * b, b), b), at], dst.at[:, at])

    clear(w.at[0:e, 0 : 2 * e])
    start_w(rel, slots, p_hbm.at[0:g], w, range(g, 2 * g), g, 0, 2 * g, s_p)
    clear(w.at[2 * e : 3 * e, e : 3 * e])
    start_w(rel, slots, p_hbm.at[2 * g : 3 * g], w, range(3 * g, 4 * g), g, g, 3 * g, s_p)
    clear(a_h)
    start_a(acol, a_hbm, a_h, range(2 * g, 3 * g), g, s_h)
    clear(a_l)
    start_a(acol, a_hbm, a_l, range(0, g), 0, s_l)
    start_w(rel, slots, p_hbm.at[g : 2 * g], w, range(2 * g, 3 * g), g, g, 2 * g, s_m)
    wait_all(p_hbm.at[0 : 2 * g], s_p)
    wait_all(a_hbm.at[0:g], s_h)
    low = w[0:e, 0:e]
    high = w[2 * e : 3 * e, 2 * e : 3 * e]
    h0_v[...] = dot(a_h[:, 0:e], low).astype(BF16)
    send(h0_v, h0_hbm)
    far[:, one] = dot_t(high, h0_v[...]).astype(BF16)
    send_far(one)
    wait_all(a_hbm.at[0:g], s_l)
    l2_v[...] = dot(a_l[:, 3 * e : 4 * e], high).astype(BF16)
    send(l2_v, l2_hbm)
    far[:, two] = dot_t(low, l2_v[...]).astype(BF16)
    send_far(two)
    corner_l[...] = low
    corner_h[...] = high
    ghost_l[...] = a_l[:, 0:e]
    ghost_h[...] = a_h[:, 3 * e : 4 * e]
    own_l[:, one] = dot(a_l[:, e : 2 * e], low)
    own_h[:, two] = dot(a_h[:, 2 * e : 3 * e], high)
    wait_all(p_hbm.at[0:g], s_m)
    own_l[:, two] = dot(a_l[:, e : 4 * e], w[:, two])
    own_h[:, one] = dot(a_h[:, 0 : 3 * e], w[:, two])
    for out in outs:
        out.wait()


def second_kernel(
    rel, slots, ghost_l, ghost_h, low, high, own_l, own_h, pair, cross, l_hbm, h_hbm, pair_hbm, cross_hbm,
    w_b, w_a, l_v, h_v, up, down, s_b, s_u, s_o,
):
    e = up.shape[0]
    g = GHOST
    one, two = slice(0, e), slice(e, 2 * e)
    even = is_even()
    outs = []

    def ghost_below(below):
        start_w(rel, slots, below, w_b, range(0, g), 0, 0, 2 * g, s_b)

    def ghost_above(above):
        start_w(rel, slots, above, w_a, range(4 * g, 5 * g), 4 * g, g, 3 * g, s_u, g)

    def by_parity(start, if_even, if_odd):
        @pl.when(even)
        def _():
            start(if_even)

        @pl.when(jnp.logical_not(even))
        def _():
            start(if_odd)

    def send(src, dst):
        outs.append(pltpu.make_async_copy(src, dst, s_o.at[len(outs)]))
        outs[-1].start()

    def send_to(src, if_even, if_odd):
        sem = s_o.at[len(outs)]
        outs.append(pltpu.make_async_copy(src, if_even, sem))

        @pl.when(even)
        def _():
            pltpu.make_async_copy(src, if_even, sem).start()

        @pl.when(jnp.logical_not(even))
        def _():
            pltpu.make_async_copy(src, if_odd, sem).start()

    clear(w_b)
    by_parity(ghost_below, cross, pair)
    clear(w_a)
    by_parity(ghost_above, pair, cross)
    wait_all(pair, s_b)
    l_v[...] = (own_l[...] + dot(ghost_l[...], w_b[...])).astype(BF16)
    send(l_v, l_hbm)
    down[...] = dot_t(low[...], l_v[...]).astype(BF16)
    send_to(down, cross_hbm, pair_hbm)
    wait_all(cross, s_u)
    h_v[:, one] = (own_h[:, one] + dot(ghost_h[...], w_a[:, one])).astype(BF16)
    up[:, one] = dot_t(high[...], h_v[:, one]).astype(BF16)
    send_to(up.at[:, one], pair_hbm.at[:, one], cross_hbm.at[:, one])
    h_v[:, two] = (own_h[:, two] + dot(ghost_h[...], w_a[:, two])).astype(BF16)
    send(h_v, h_hbm)
    for at in (slice(e, e + e // 2), slice(e + e // 2, 2 * e)):
        up[:, at] = dot_t(high[...], h_v[:, at]).astype(BF16)
        send_to(up.at[:, at], pair_hbm.at[:, at], cross_hbm.at[:, at])
    for out in outs:
        out.wait()


def third_kernel(
    acol, rel, slots, a_hbm, p_hbm, l_hbm, h_hbm, l2_hbm, h0_hbm, middle, a_m, ap_l, ap_m, ap_h, w, s_p, s_m, s_a
):
    e = a_m.shape[0]
    g = GHOST
    clear(w.at[0:e, 0 : 2 * e])
    start_w(rel, slots, p_hbm.at[0:g], w, range(g, 2 * g), g, 0, 2 * g, s_p)
    clear(w.at[2 * e : 3 * e, e : 3 * e])
    start_w(rel, slots, p_hbm.at[2 * g : 3 * g], w, range(3 * g, 4 * g), g, g, 3 * g, s_p)
    start_w(rel, slots, p_hbm.at[g : 2 * g], w, range(2 * g, 3 * g), g, g, 2 * g, s_p)
    clear(a_m)
    start_a(acol, a_hbm, a_m, range(g, 2 * g), g, s_m)
    moves = [
        pltpu.make_async_copy(src, dst, s_a.at[i])
        for i, (src, dst) in enumerate(
            (
                (l_hbm, ap_l.at[:, 0 : 2 * e]),
                (l2_hbm, ap_l.at[:, 2 * e : 3 * e]),
                (h0_hbm, ap_h.at[:, 0:e]),
                (h_hbm, ap_h.at[:, e : 3 * e]),
            )
        )
    ]
    for move in moves:
        move.start()
    wait_all(p_hbm, s_p)
    wait_all(a_hbm.at[g : 2 * g], s_m)
    ap_m[:, 0:e] = dot(a_m[:, 0:e], w[0:e, 0:e]).astype(BF16)
    ap_m[:, e : 2 * e] = dot(a_m[...], w[:, e : 2 * e]).astype(BF16)
    ap_m[:, 2 * e : 3 * e] = dot(a_m[:, 2 * e : 3 * e], w[2 * e : 3 * e, 2 * e : 3 * e]).astype(BF16)
    for move in moves:
        move.wait()
    w_l = w[0:e, e : 2 * e]
    w_m = w[e : 2 * e, e : 2 * e]
    w_h = w[2 * e : 3 * e, e : 2 * e]
    for c in range(3):
        at = slice(c * e, (c + 1) * e)
        middle[:, at] = dot_t(w_l, ap_l[:, at]) + dot_t(w_m, ap_m[:, at]) + dot_t(w_h, ap_h[:, at])


def fourth_kernel(middle, pair, cross, own, *refs):
    count = len(refs) // 2
    outs, (*nears, s_o) = refs[:count], refs[count:]
    b = own.shape[0]
    e = pair.shape[0]
    one, two, three = (slice(c * e, (c + 1) * e) for c in range(3))
    even = is_even()
    plane = lax.axis_index("plane")

    def join(below, above):
        for d in OTHERS + (0,):
            rows = pl.ds(pl.multiple_of((plane ^ d) * b, b), b)
            to = nears[OTHERS.index(d)] if d else own
            to[:, one] = (middle[rows, one] + below[rows, one].astype(F32)).astype(to.dtype)
            total = middle[rows, two] + below[rows, two].astype(F32) + above[rows, one].astype(F32)
            to[:, two] = total.astype(to.dtype)
            to[:, three] = (middle[rows, three] + above[rows, two].astype(F32)).astype(to.dtype)
            if d:
                k = OTHERS.index(d)
                pltpu.make_async_copy(nears[k], outs[k], s_o.at[k]).start()

    @pl.when(even)
    def _():
        join(cross, pair)

    @pl.when(jnp.logical_not(even))
    def _():
        join(pair, cross)

    for k in range(count):
        pltpu.make_async_copy(nears[k], outs[k], s_o.at[k]).wait()


def summed_kernel(*refs):
    *fars, low, high = refs
    e = low.shape[1]
    low[...] = sum(far[:, 0:e].astype(F32) for far in fars)
    high[...] = sum(far[:, e : 2 * e].astype(F32) for far in fars)


def run(body, ins, in_specs, outs, out_specs, scratch, flops):
    return pl.pallas_call(
        body,
        in_specs=in_specs,
        out_specs=out_specs,
        out_shape=outs,
        scratch_shapes=scratch,
        compiler_params=pltpu.CompilerParams(vmem_limit_bytes=VMEM_LIMIT),
        cost_estimate=pl.CostEstimate(flops=flops, transcendentals=0, bytes_accessed=8 * 1024 * 1024),
    )(*ins)


def swapped(shard, first):
    count = lax.axis_size("slab")
    pairs = [(i, i + 1) for i in range(first, count - 1, 2)]
    return lax.ppermute(shard, "slab", pairs + [(j, i) for i, j in pairs])


def over_planes(shard, d):
    return lax.ppermute(shard, "plane", [(q, q ^ d) for q in range(lax.axis_size("plane"))])


def passed_along(shard, by):
    count = lax.axis_size("slab")
    pairs = [(i, i + by) for i in range(count) if 0 <= i + by < count]
    return lax.ppermute(shard, "slab", pairs)


def window_cols(p_cols, coarse_slot, rows_here):
    coarse = coarse_slot.shape[1]
    slab = lax.axis_index("slab")
    column = lax.axis_index("plane")
    turned = jnp.transpose(p_cols, (0, 2, 1))
    mine = lax.dynamic_slice_in_dim(turned, column, 1, 0)[0]
    mine = jnp.pad(mine, ((0, 0), (GHOST, GHOST)))
    near = lax.dynamic_slice_in_dim(mine, slab * rows_here, rows_here + 2 * GHOST, 1)
    slots = jnp.pad(coarse_slot, ((1, 1), (0, 0)))
    return near - (slab - 1) * coarse, lax.dynamic_slice_in_dim(slots, slab, 3, 0)


def steps(a_blocks, a_cols, p_blocks, p_cols, coarse_slot):
    rows_here, b = a_blocks.shape[1], a_blocks.shape[3]
    coarse = coarse_slot.shape[1]
    e = coarse * b
    slab = lax.axis_index("slab")
    a, p = a_blocks[0], p_blocks[0]
    a = pltpu.with_memory_space_constraint(a, pltpu.HBM)
    p_here = pltpu.with_memory_space_constraint(p, pltpu.HBM)
    part = pltpu.VMEM((GHOST, *p.shape[1:]), BF16)
    pair, cross = run(halo_kernel, (p_here,), [HBM], (part, part), (VMEM, VMEM), [pltpu.SemaphoreType.DMA((2,))], 0)
    cross = swapped(cross, 1)
    pair = swapped(pair, 0)
    rel, slots = window_cols(p_cols, coarse_slot, rows_here)
    acol = a_cols[0] - (slab * rows_here - GHOST)
    unit = 2 * e * e * b

    def shape(rows, cols, dtype=BF16, space=pltpu.VMEM):
        return space((rows * e, cols * e), dtype)

    def far_shape(rows, cols):
        return shape(rows, cols, BF16, pltpu.HBM)

    a = pltpu.with_memory_space_constraint(a, pltpu.HBM)
    p_here = pltpu.with_memory_space_constraint(p, pltpu.HBM)

    def scratch(rows, cols):
        return pltpu.VMEM((rows * e, cols * e), BF16)

    dma = pltpu.SemaphoreType.DMA(())
    ghost_l, ghost_h, corner_l, corner_h, own_l, own_h, ap_h0, ap_l2, *fars = run(
        first_kernel,
        (acol, rel, slots, a, p_here),
        [SMEM, SMEM, SMEM, HBM, HBM],
        (shape(1, 1),) * 4 + (shape(1, 2, F32),) * 2 + (far_shape(1, 1), far_shape(1, 1)) + (pltpu.HBM((b, 2 * e), BF16),) * (1 + len(OTHERS)),
        (VMEM,) * 6 + (HBM,) * (3 + len(OTHERS)),
        [scratch(1, 4), scratch(1, 4), scratch(3, 3), scratch(1, 1), scratch(1, 1), scratch(1, 2)]
        + [dma] * 4
        + [pltpu.SemaphoreType.DMA((2 + 2 * (1 + len(OTHERS)),))],
        48 * unit,
    )
    for k, d in enumerate(OTHERS):
        fars[1 + k] = over_planes(fars[1 + k], d)
    pair, cross = (pltpu.with_memory_space_constraint(x, pltpu.VMEM) for x in (pair, cross))
    ap_l, ap_h, pair, cross = run(
        second_kernel,
        (rel, slots, ghost_l, ghost_h, corner_l, corner_h, own_l, own_h, pair, cross),
        [SMEM, SMEM] + [VMEM] * 8,
        (far_shape(1, 2),) * 4,
        (HBM,) * 4,
        [scratch(1, 2)] * 6 + [dma, dma, pltpu.SemaphoreType.DMA((6,))],
        32 * unit,
    )
    cross = swapped(cross, 1)
    pair = swapped(pair, 0)
    kept = tuple(pltpu.with_memory_space_constraint(x, pltpu.HBM) for x in (ap_l, ap_h, ap_l2, ap_h0))
    middle = run(
        third_kernel,
        (acol, rel, slots, a, p_here) + kept,
        [SMEM, SMEM, SMEM] + [HBM] * 6,
        shape(1, 3, F32),
        VMEM,
        [scratch(1, 3)] * 4 + [scratch(3, 3), dma, dma, pltpu.SemaphoreType.DMA((4,))],
        56 * unit,
    )
    chunk = ((b, 3 * e), BF16)
    own, *nears = run(
        fourth_kernel,
        (middle, pair, cross),
        [VMEM] * 3,
        (pltpu.VMEM((b, 3 * e), F32),) + (pltpu.HBM(*chunk),) * len(OTHERS),
        (VMEM,) + (HBM,) * len(OTHERS),
        [pltpu.VMEM(*chunk)] * len(OTHERS) + [pltpu.SemaphoreType.DMA((len(OTHERS),))],
        e * 3 * e,
    )
    got = []
    for k, d in enumerate(OTHERS):
        got.append(over_planes(nears[k], d))
    one = pltpu.VMEM((b, e), F32)
    low, high = run(summed_kernel, tuple(fars), [VMEM] * len(fars), (one, one), (VMEM, VMEM), [], b * e * 8)
    far_low = passed_along(low, 1)
    far_high = passed_along(high, -1)
    near = (own + sum(x.astype(F32) for x in got))[None]
    return jnp.concatenate([far_low[None], near, far_high[None]], axis=2)[None]


def solution(mesh):
    return jax.shard_map(
        steps,
        mesh=mesh,
        in_specs=(
            P("plane", "slab", None, None, None),
            P("plane", "slab", None),
            P("plane", "slab", None, None, None),
            P(),
            P(),
        ),
        out_specs=P("plane", "slab", None, None),
        check_vma=False,
    )
```
